256 devices in a mesh: body: 2 (over x_hi), gx: 32 (over y, z), yz: 4 (over x_lo, core).
Axes of the slice: x: 4 (x_hi: 2, x_lo: 2; x = x_hi * 2 + x_lo), y: 4, z: 8, core: 2. Of those that a mesh axis runs over, the one named last changes fastest.
Arguments:
- displacement: float32 [2, 3, 512, 256, 128], P('body', None, 'gx', 'yz'), may hold values from -1.75 to 1.75
- velocity: float32 [2, 3, 512, 256, 128], P('body', None, 'gx', 'yz'), may hold values from -3 to 3
- material: int32 [2, 512, 256, 128], P('body', 'gx', 'yz'), may hold values from 0 to 7
- moduli: float32 [8], replicated, may hold values from 0.5 to 2
- density: float32 [8], replicated, may hold values from 1 to 4
- partner: int32 [256], replicated, may hold values from 0 to 255, as said below
- active: int32 [256], replicated, may hold values 0 or 1
Outputs:
- final_displacement: float32 [2, 3, 512, 256, 128], P('body', None, 'gx', 'yz')
- final_velocity: float32 [2, 3, 512, 256, 128], P('body', None, 'gx', 'yz')
The draws below stay inside these ranges and needn't reach their ends.
Inputs may be any that keep to these rules, and one draw needn't show every extreme that they name: partner is a permutation of the rows of body 1's face; in every aligned block of 64 rows of partner, exactly 32 values lie in the same-numbered block of 64 rows and the others in the next block, the last block's next being the first.
All inputs are finite; a program needn't handle non-finite values.
Results may differ from the reference program's by a relative error of at most 0.0001.
Values sent between devices are 32-bit elements; how exact they have to be, the bound alone decides.
A program may use at most 64 MiB of HBM per device.

```python
import math
import jax
import jax.numpy as jnp
from jax import lax

CY = 64
NZ = 128
STEPS = 4
MATS = 8
NX = 512
NY = 256


def draw_partner(key, part):
    blocks = NY // CY
    half_rows = CY // 2
    row_keys = jax.random.split(jax.random.fold_in(key, 7), 2 * blocks)
    starting = jax.vmap(lambda subkey: jax.random.permutation(subkey, CY))(row_keys[:blocks])
    starting = starting + (jnp.arange(blocks) * CY)[:, None]
    joined = jnp.concatenate([starting[:, :half_rows], jnp.roll(starting, -1, axis=0)[:, half_rows:]], axis=1)
    orders = jax.vmap(lambda subkey: jax.random.permutation(subkey, CY))(row_keys[blocks:])
    mixed = jnp.take_along_axis(joined, orders, axis=1)
    return mixed.reshape(NY).astype(jnp.int32)


def set_ends(entries, key, smallest, largest):
    place = [jax.random.randint(jax.random.fold_in(key, axis), (), 0, length) for axis, length in enumerate(entries.shape)]
    widest = entries.shape.index(max(entries.shape))
    next_to = place[:widest] + [(place[widest] + 1) % entries.shape[widest]] + place[widest + 1:]
    return entries.at[tuple(place)].set(smallest).at[tuple(next_to)].set(largest)


def levels(key, shape, pieces, least, high):
    level = 1.0
    for dim, parts in pieces:
        draws = jax.random.uniform(jax.random.fold_in(jax.random.fold_in(key, 6), dim), (parts,), jnp.float32, least / len(pieces), high / len(pieces))
        level = level * jnp.repeat(jnp.exp(draws), shape[dim] // parts).reshape((-1,) + (1,) * (len(shape) - 1 - dim))
    return level


def noise(rng, shape, deviation, limit, shards=(), kind=jnp.bfloat16):
    factor_of = levels(rng, shape, shards, -0.22, 0.18) if shards else 1.0
    values = jax.random.normal(rng, shape, jnp.float32) * deviation * factor_of
    return jnp.minimum(jnp.maximum(values, -limit), limit).astype(kind)


def setup_inputs(seed: int = 0) -> dict:
    key_list = jax.random.split(jax.random.key(seed), 8)
    return {
        "displacement": noise(key_list[0], (2, 3, NX, NY, NZ), 0.3, 1.75, ((0, 2), (2, 32), (3, 4)), jnp.float32),
        "velocity": noise(key_list[1], (2, 3, NX, NY, NZ), 0.5, 3.0, ((0, 2), (2, 32), (3, 4)), jnp.float32),
        "material": set_ends(jax.random.randint(key_list[2], (2, NX, NY, NZ), 0, MATS), jax.random.fold_in(key_list[2], 1), 0, MATS - 1).astype(jnp.int32),
        "moduli": jnp.clip(jnp.exp(jax.random.uniform(key_list[3], (MATS,), jnp.float32, math.log(0.5), math.log(2.0))), 0.5, 2.0),
        "density": jnp.clip(jnp.exp(jax.random.uniform(key_list[4], (MATS,), jnp.float32, math.log(1.0), math.log(4.0))), 1.0, 4.0),
        "partner": draw_partner(jax.random.fold_in(key_list[7], 71), 0),
        "active": set_ends((jax.random.randint(key_list[6], (NY,), 0, 4) < 3).astype(jnp.int32), jax.random.fold_in(key_list[6], 1), 0, 1),
    }


STEP_TIME = 0.2
YIELD_SPAN = 0.5
PENALTY = 4.0
SOFT_WIDTH = 0.1
KERNEL_WIDTH = 1.5


def tension(stretch):
    return YIELD_SPAN * jnp.tanh(stretch / YIELD_SPAN)


def pair_pressure(own_surface, far_surface):
    column = jnp.arange(own_surface.shape[-1]).astype(jnp.float32)
    opening = -own_surface[0][:, :, None] - far_surface[0][:, None, :]
    along_z = (column + own_surface[2])[:, :, None] - (column + far_surface[2])[:, None, :]
    along_y = own_surface[1][:, :, None] - far_surface[1][:, None, :]
    weight = jnp.exp(-(along_y * along_y + along_z * along_z) / (2.0 * KERNEL_WIDTH * KERNEL_WIDTH))
    return weight * (PENALTY * SOFT_WIDTH) * jax.nn.softplus(-opening / SOFT_WIDTH)


def axis_forces(displace, stiffness, dimension):
    extent = displace.shape[dimension]
    zero_plane = jnp.zeros_like(lax.slice_in_dim(displace, 0, 1, axis=dimension))
    ahead = jnp.concatenate([lax.slice_in_dim(displace, 1, extent, axis=dimension), zero_plane], axis=dimension)
    pulls = stiffness * tension(ahead - displace)
    behind = jnp.concatenate([zero_plane, lax.slice_in_dim(pulls, 0, extent - 1, axis=dimension)], axis=dimension)
    return pulls - behind


def reference(displacement, velocity, material, moduli, density, partner, active):
    inside = ((jnp.arange(NX) < NX - 1)[:, None, None]
              & (jnp.arange(NY) < NY - 1)[None, :, None]
              & (jnp.arange(NZ) < NZ - 1)[None, None, :])
    elements = jnp.where(inside[None], moduli[material], 0.0)
    node_mass = density[material][:, None]
    padded = jnp.pad(elements, ((0, 0), (1, 0), (1, 0), (1, 0)))
    stiff_x = 0.25 * (padded[:, 1:, 1:, 1:] + padded[:, 1:, :-1, 1:] + padded[:, 1:, 1:, :-1] + padded[:, 1:, :-1, :-1])
    stiff_y = 0.25 * (padded[:, 1:, 1:, 1:] + padded[:, :-1, 1:, 1:] + padded[:, 1:, 1:, :-1] + padded[:, :-1, 1:, :-1])
    stiff_z = 0.25 * (padded[:, 1:, 1:, 1:] + padded[:, :-1, 1:, 1:] + padded[:, 1:, :-1, 1:] + padded[:, :-1, :-1, 1:])
    active_rows = active.astype(jnp.float32)[:, None]
    for repeat in range(STEPS):
        forces = axis_forces(displacement, stiff_x[:, None], 2)
        forces = forces + axis_forces(displacement, stiff_y[:, None], 3)
        forces = forces + axis_forces(displacement, stiff_z[:, None], 4)
        own_surface = displacement[0, :, NX - 1]
        far_surface = displacement[1, :, NX - 1]
        matched = jnp.take(far_surface, partner, axis=1)
        pressure = pair_pressure(own_surface, matched)
        pushes = -jnp.sum(pressure, axis=2) * active_rows
        reaction = -jnp.sum(pressure, axis=1) * active_rows
        placed = jnp.zeros((NY, NZ), jnp.float32).at[partner].add(reaction)
        forces = forces.at[0, 0, NX - 1].add(pushes)
        forces = forces.at[1, 0, NX - 1].add(placed)
        velocity = velocity + STEP_TIME * forces / node_mass
        displacement = displacement + STEP_TIME * velocity
    return displacement, velocity
```

```python
import functools
import math

import jax
import jax.numpy as jnp
from jax import lax
from jax.experimental import pallas as pl
from jax.experimental.pallas import tpu as pltpu
from jax.sharding import PartitionSpec as P

STEPS = 4
STEP_TIME = 0.2
YIELD_SPAN = 0.5
PENALTY = 4.0
SOFT_WIDTH = 0.1
KERNEL_WIDTH = 1.5
LOG2E = 1.0 / math.log(2.0)
PLANE = math.sqrt(LOG2E / (2.0 * KERNEL_WIDTH * KERNEL_WIDTH))
GROUP = 8

MESH = pl.DeviceIdType.MESH
HIGHEST = lax.Precision.HIGHEST


def kernel(
    count_x, count_y, dims,
    disp, velo, mat_hbm, moduli, density, partner, active,
    out_d, out_v,
    D, V, M, E, SX, SY, SYL, SZ, C,
    XH, YH, YS, MX, MY, MC, MYS, CP, G, GT, ACT, WT, FX,
    load_sem, out_sem, m_send, m_recv, x_send, x_recv, y_send, y_recv, c_send, c_recv,
):
    length_x, length_y, length_z = dims
    last = length_x - 1
    body = lax.axis_index("body")
    gx = lax.axis_index("gx")
    yz = lax.axis_index("yz")
    has_lo = gx > 0
    has_hi = gx < count_x - 1
    has_dn = yz > 0
    has_up = yz < count_y - 1
    is_face = gx == count_x - 1
    cross = lax.rem(yz + 1 - 2 * body + count_y, count_y)
    other = 1 - body

    low = {"gx": gx - 1}
    high = {"gx": gx + 1}
    down = {"yz": yz - 1}
    up = {"yz": yz + 1}
    corner_up = {"gx": gx + 1, "yz": yz + 1}
    corner_dn = {"gx": gx - 1, "yz": yz - 1}
    same_peer = {"body": other}
    cross_peer = {"body": other, "yz": cross}

    row_id = lax.broadcasted_iota(jnp.int32, (length_y, length_z), 0)
    lane_id = lax.broadcasted_iota(jnp.int32, (length_y, length_z), 1)

    loads = [
        pltpu.make_async_copy(mat_hbm.at[0], M, load_sem.at[0]),
        pltpu.make_async_copy(disp.at[0], D.at[0], load_sem.at[1]),
        pltpu.make_async_copy(velo.at[0], V, load_sem.at[2]),
    ]
    for item in loads:
        item.start()

    barrier = pltpu.get_barrier_semaphore()

    def greet(condition, device):
        @pl.when(condition)
        def _():
            pl.semaphore_signal(barrier, inc=1, device_id=device, device_id_type=MESH)

    pairs = [
        (has_lo, low), (has_hi, high), (has_dn, down), (has_up, up),
        (has_hi & has_up, corner_up), (has_lo & has_dn, corner_dn),
        (is_face, same_peer), (is_face, cross_peer),
    ]
    for condition, device in pairs:
        greet(condition, device)
    pl.semaphore_wait(barrier, sum(condition.astype(jnp.int32) for condition, _ in pairs))

    def remote(source, target, send, recv, device):
        return pltpu.make_async_remote_copy(
            src_ref=source, dst_ref=target, send_sem=send, recv_sem=recv,
            device_id=device, device_id_type=MESH,
        )

    def x_up(s, source):
        return remote(source, XH.at[s, 0], x_send.at[s, 0], x_recv.at[s, 0], high)

    def x_down(s, source):
        return remote(source, XH.at[s, 1], x_send.at[s, 1], x_recv.at[s, 1], low)

    def y_up(s):
        return remote(YS.at[s, 0], YH.at[s, 0], y_send.at[s, 0], y_recv.at[s, 0], up)

    def y_down(s):
        return remote(YS.at[s, 1], YH.at[s, 1], y_send.at[s, 1], y_recv.at[s, 1], down)

    def c_same(s, c, source):
        return remote(source, CP.at[s, c, 0], c_send.at[s, c, 0], c_recv.at[s, c, 0], same_peer)

    def c_cross(s, c, source):
        return remote(source, CP.at[s, c, 1], c_send.at[s, c, 1], c_recv.at[s, c, 1], cross_peer)

    m_x = remote(mat_hbm.at[0, last], MX, m_send.at[0], m_recv.at[0], high)
    m_y = remote(MYS, MY, m_send.at[1], m_recv.at[1], up)
    m_c = remote(MYS.at[pl.ds(length_x - 8, 8)], MC, m_send.at[2], m_recv.at[2], corner_up)

    @pl.when(has_hi)
    def _():
        m_x.start()
        x_up(0, disp.at[0, :, last]).start()

    @pl.when(has_lo)
    def _():
        x_down(0, disp.at[0, :, 0]).start()

    @pl.when(is_face)
    def _():
        for c in (1, 2, 0):
            c_same(0, c, disp.at[0, c, last]).start()
            c_cross(0, c, disp.at[0, c, last]).start()

    @pl.when(jnp.logical_not(has_lo))
    def _():
        XH[:, 0] = jnp.zeros((STEPS, 3, length_y, length_z), jnp.float32)

    @pl.when(jnp.logical_not(has_hi))
    def _():
        XH[:, 1] = jnp.zeros((STEPS, 3, length_y, length_z), jnp.float32)

    @pl.when(jnp.logical_not(has_dn))
    def _():
        YH[:, 0] = jnp.zeros((STEPS, 3, length_x, length_z), jnp.float32)
        MY[...] = jnp.zeros((length_x, length_z), jnp.int32)

    @pl.when(jnp.logical_not(has_up))
    def _():
        YH[:, 1] = jnp.zeros((STEPS, 3, length_x, length_z), jnp.float32)

    @pl.when(jnp.logical_not(has_lo))
    def _():
        MX[...] = jnp.zeros((length_y, length_z), jnp.int32)

    @pl.when(jnp.logical_not(has_lo & has_dn))
    def _():
        MC[...] = jnp.zeros((8, length_z), jnp.int32)

    loads[0].wait()

    @pl.loop(0, length_x)
    def _(i):
        MYS[pl.ds(i, 1)] = M[i, pl.ds(length_y - 1, 1)]

    @pl.when(has_up)
    def _():
        m_y.start()

    @pl.when(has_hi & has_up)
    def _():
        m_c.start()

    loads[1].wait()

    @pl.loop(0, length_x)
    def _(i):
        for c in range(3):
            YS[0, 0, c, pl.ds(i, 1)] = D[0, c, i, pl.ds(length_y - 1, 1)]
            YS[0, 1, c, pl.ds(i, 1)] = D[0, c, i, pl.ds(0, 1)]

    @pl.when(has_up)
    def _():
        y_up(0).start()

    @pl.when(has_dn)
    def _():
        y_down(0).start()

    def lookup(kinds, table):
        result = jnp.full(kinds.shape, table[0], jnp.float32)
        for kind in range(1, 8):
            result = jnp.where(kinds == kind, table[kind], result)
        return result

    inner_lane = lane_id < length_z - 1
    own_edge = inner_lane & jnp.logical_or(has_up, row_id < length_y - 1)

    @pl.loop(0, length_x)
    def _(i):
        kinds = M[i]
        keep = own_edge & (jnp.logical_or(has_hi, i < last))
        E[i + 1, pl.ds(8, length_y)] = jnp.where(keep, lookup(kinds, moduli), 0.0)
        C[i] = STEP_TIME / lookup(kinds, density)

    @pl.when(is_face)
    def _():
        base = yz * length_y
        side_base = cross * length_y
        pool_lane = lax.broadcasted_iota(jnp.int32, (1, 2 * length_y), 1)

        @pl.when(body == 0)
        def _():
            @pl.loop(0, length_y)
            def _(r):
                wanted = partner[base + r]
                column = jnp.where(
                    (wanted >= base) & (wanted < base + length_y),
                    wanted - base,
                    wanted - side_base + length_y,
                )
                G[pl.ds(r, 1)] = jnp.where(pool_lane == column, 1.0, 0.0)
                ACT[pl.ds(r, 1)] = jnp.full((1, length_z), active[base + r].astype(jnp.float32))

        @pl.when(body == 1)
        def _():
            @pl.loop(0, 2 * length_y)
            def _(q):
                row = jnp.where(q < length_y, base + q, side_base + q - length_y)
                GT[pl.ds(q, 1)] = jnp.where(pool_lane == partner[row] - base, 1.0, 0.0)
                FX[pl.ds(q, 1)] = jnp.full((1, length_z), active[row].astype(jnp.float32))

            turned = GT[...].T[:length_y]
            G[...] = turned
            ACT[...] = jnp.dot(turned, FX[...], preferred_element_type=jnp.float32, precision=HIGHEST)

    @pl.when(has_lo)
    def _():
        m_x.wait_recv()

    @pl.when(has_dn)
    def _():
        m_y.wait_recv()

    @pl.when(has_lo & has_dn)
    def _():
        m_c.wait_recv()

    E[0, pl.ds(8, length_y)] = jnp.where(own_edge & has_lo, lookup(MX[...], moduli), 0.0)
    row_lane = lax.broadcasted_iota(jnp.int32, (length_x, length_z), 1) < length_z - 1
    row_pos = lax.broadcasted_iota(jnp.int32, (length_x, length_z), 0)
    side = jnp.where(
        row_lane & has_dn & jnp.logical_or(has_hi, row_pos < last), lookup(MY[...], moduli), 0.0
    )
    SYL[...] = side
    E[0, pl.ds(7, 1)] = jnp.where(
        inner_lane[:1] & has_lo & has_dn, lookup(MC[pl.ds(7, 1)], moduli), 0.0
    )

    @pl.loop(0, length_x)
    def _(i):
        E[i + 1, pl.ds(7, 1)] = SYL[pl.ds(i, 1)]

    def with_left(value):
        return value + pltpu.roll(value, 1, 1)

    quarter = 0.25 * YIELD_SPAN

    @pl.loop(0, length_x + 1)
    def _(i):
        whole = E[i]
        here = whole[8:]
        behind = pltpu.roll(whole, 1, 0)[8:]
        SX[i] = quarter * with_left(here + behind)

        @pl.when(i > 0)
        def _():
            under = E[i - 1]
            both = whole + under
            SY[i - 1] = quarter * with_left(both[8:])
            SZ[i - 1] = quarter * (both + pltpu.roll(both, 1, 0))[8:]
            SYL[pl.ds(i - 1, 1)] = quarter * with_left(both[7:8])

    loads[2].wait()

    sharp = 1.0 / YIELD_SPAN

    def scaled(s, c, x):
        return D[s, c, x] * sharp

    def node_update(s, c, x, here, pull_x, pull_x_below, extra):
        ahead = pltpu.roll(here, length_y - 1, 0)
        ahead = jnp.where(row_id == length_y - 1, YH[s, 1, c, pl.ds(x, 1)] * sharp, ahead)
        pull_y = SY[x] * jnp.tanh(ahead - here)
        first = SYL[pl.ds(x, 1)] * jnp.tanh(here[:1] - YH[s, 0, c, pl.ds(x, 1)] * sharp)
        below = jnp.where(row_id == 0, first, pltpu.roll(pull_y, 1, 0))
        pull_z = SZ[x] * jnp.tanh(pltpu.roll(here, length_z - 1, 1) - here)
        force = (pull_x - pull_x_below) + (pull_y - below) + (pull_z - pltpu.roll(pull_z, 1, 1))
        if extra is not None:
            force = force + extra
        speed = V[c, x] + C[x] * force
        V[c, x] = speed
        moved = D[s, c, x] + STEP_TIME * speed
        D[s + 1, c, x] = moved
        return moved

    def keep_rows(s, c, x, moved):
        @pl.when(s + 1 < STEPS)
        def _():
            YS[s + 1, 0, c, pl.ds(x, 1)] = moved[length_y - 1 :]
            YS[s + 1, 1, c, pl.ds(x, 1)] = moved[:1]

    def first_layer(s, c):
        here = scaled(s, c, 0)
        pull_below = SX[0] * jnp.tanh(here - XH[s, 0, c] * sharp)
        pull_x = SX[1] * jnp.tanh(scaled(s, c, 1) - here)
        keep_rows(s, c, 0, node_update(s, c, 0, here, pull_x, pull_below, None))

    def last_layer(s, c, extra=None):
        here = scaled(s, c, last)
        pull_below = SX[last] * jnp.tanh(here - scaled(s, c, last - 1))
        pull_x = SX[last + 1] * jnp.tanh(XH[s, 1, c] * sharp - here)
        keep_rows(s, c, last, node_update(s, c, last, here, pull_x, pull_below, extra))

    def matched(s, c):
        pool = CP[s, c].reshape(2 * length_y, length_z)
        return jnp.dot(G[...], pool, preferred_element_type=jnp.float32, precision=HIGHEST)

    column = lane_id.astype(jnp.float32)
    depth = LOG2E / SOFT_WIDTH

    def weights(s):
        own_y = D[s, 1, last] * PLANE
        own_z = (D[s, 2, last] + column) * PLANE
        far_y = matched(s, 1) * PLANE
        far_z = (matched(s, 2) + column) * PLANE

        @pl.loop(0, length_z // GROUP)
        def _(block):
            for k in range(GROUP):
                turn = block * GROUP + k
                along_y = own_y - pltpu.roll(far_y, turn, 1)
                along_z = own_z - pltpu.roll(far_z, turn, 1)
                WT[turn] = jnp.exp2(-(along_y * along_y + along_z * along_z))

    def contact(s):
        own_x = D[s, 0, last] * depth
        far_x = matched(s, 0) * depth

        def group(block, total):
            for k in range(GROUP):
                turn = block * GROUP + k
                squeeze = own_x + pltpu.roll(far_x, turn, 1)
                hard = jnp.maximum(squeeze, 0.0)
                soft = jnp.log(1.0 + jnp.exp2(squeeze - (hard + hard)))
                total = total + WT[turn] * (hard * math.log(2.0) + soft)
            return total

        total = lax.fori_loop(
            0, length_z // GROUP, group, jnp.zeros((length_y, length_z), jnp.float32)
        )
        return total * (ACT[...] * (-PENALTY * SOFT_WIDTH))

    def step(s, carry):
        more = s + 1 < STEPS

        @pl.when(is_face)
        def _():
            for c in (1, 2):
                c_same(s, c, D.at[s, c, last]).wait_recv()
                c_cross(s, c, D.at[s, c, last]).wait_recv()
            weights(s)

        @pl.when(has_dn)
        def _():
            y_up(s).wait_recv()

        @pl.when(has_up)
        def _():
            y_down(s).wait_recv()

        @pl.when(has_hi)
        def _():
            x_down(s, D.at[s, :, 0]).wait_recv()
            for c in range(3):
                last_layer(s, c)

            @pl.when(more)
            def _():
                x_up(s + 1, D.at[s + 1, :, last]).start()

        @pl.when(is_face)
        def _():
            for c in (1, 2):
                last_layer(s, c)

                @pl.when(more)
                def _():
                    c_same(s + 1, c, D.at[s + 1, c, last]).start()
                    c_cross(s + 1, c, D.at[s + 1, c, last]).start()

        @pl.when(has_lo)
        def _():
            x_up(s, D.at[s, :, last]).wait_recv()

        for c in range(3):
            first_layer(s, c)

        @pl.when(more & has_lo)
        def _():
            x_down(s + 1, D.at[s + 1, :, 0]).start()

        for c in range(3):
            here = scaled(s, c, 1)
            pull = SX[1] * jnp.tanh(here - scaled(s, c, 0))

            def layer(x, state):
                here, below = state
                ahead = scaled(s, c, x + 1)
                pull_x = SX[x + 1] * jnp.tanh(ahead - here)
                keep_rows(s, c, x, node_update(s, c, x, here, pull_x, below, None))
                return ahead, pull_x

            lax.fori_loop(1, last, layer, (here, pull))

        @pl.when(is_face)
        def _():
            c_same(s, 0, D.at[s, 0, last]).wait_recv()
            c_cross(s, 0, D.at[s, 0, last]).wait_recv()
            last_layer(s, 0, contact(s))

            @pl.when(more)
            def _():
                c_same(s + 1, 0, D.at[s + 1, 0, last]).start()
                c_cross(s + 1, 0, D.at[s + 1, 0, last]).start()

        @pl.when(more & has_up)
        def _():
            y_up(s + 1).start()

        @pl.when(more & has_dn)
        def _():
            y_down(s + 1).start()

        return carry

    lax.fori_loop(0, STEPS, step, 0)

    stores = [
        pltpu.make_async_copy(D.at[STEPS], out_d.at[0], out_sem.at[0]),
        pltpu.make_async_copy(V, out_v.at[0], out_sem.at[1]),
    ]
    for item in stores:
        item.start()

    @pl.when(has_hi)
    def _():
        m_x.wait_send()

    @pl.when(has_up)
    def _():
        m_y.wait_send()

    @pl.when(has_hi & has_up)
    def _():
        m_c.wait_send()

    def drain(s, carry):
        @pl.when(has_hi)
        def _():
            x_up(s, D.at[s, :, last]).wait_send()

        @pl.when(has_lo)
        def _():
            x_down(s, D.at[s, :, 0]).wait_send()

        @pl.when(has_up)
        def _():
            y_up(s).wait_send()

        @pl.when(has_dn)
        def _():
            y_down(s).wait_send()

        @pl.when(is_face)
        def _():
            for c in range(3):
                c_same(s, c, D.at[s, c, last]).wait_send()
                c_cross(s, c, D.at[s, c, last]).wait_send()

        return carry

    lax.fori_loop(0, STEPS, drain, 0)
    for item in stores:
        item.wait()


def local(displacement, velocity, material, moduli, density, partner, active):
    length_x, length_y, length_z = displacement.shape[2:]
    count_x = lax.axis_size("gx")
    count_y = lax.axis_size("yz")
    f32 = jnp.float32
    i32 = jnp.int32
    layer = (length_y, length_z)
    solid = (length_x,) + layer
    anywhere = pl.BlockSpec(memory_space=pl.ANY)
    scalars = pl.BlockSpec(memory_space=pltpu.SMEM)
    dma = pltpu.SemaphoreType.DMA
    return pl.pallas_call(
        functools.partial(kernel, count_x, count_y, (length_x, length_y, length_z)),
        out_shape=(
            jax.ShapeDtypeStruct(displacement.shape, f32),
            jax.ShapeDtypeStruct(velocity.shape, f32),
        ),
        in_specs=[anywhere] * 3 + [scalars] * 4,
        out_specs=(anywhere, anywhere),
        scratch_shapes=[
            pltpu.VMEM((STEPS + 1, 3) + solid, f32),
            pltpu.VMEM((3,) + solid, f32),
            pltpu.VMEM(solid, i32),
            pltpu.VMEM((length_x + 1, length_y + 8, length_z), f32),
            pltpu.VMEM((length_x + 1,) + layer, f32),
            pltpu.VMEM(solid, f32),
            pltpu.VMEM((length_x, length_z), f32),
            pltpu.VMEM(solid, f32),
            pltpu.VMEM(solid, f32),
            pltpu.VMEM((STEPS, 2, 3) + layer, f32),
            pltpu.VMEM((STEPS, 2, 3, length_x, length_z), f32),
            pltpu.VMEM((STEPS, 2, 3, length_x, length_z), f32),
            pltpu.VMEM(layer, i32),
            pltpu.VMEM((length_x, length_z), i32),
            pltpu.VMEM((8, length_z), i32),
            pltpu.VMEM((length_x, length_z), i32),
            pltpu.VMEM((STEPS, 3, 2) + layer, f32),
            pltpu.VMEM((length_y, 2 * length_y), f32),
            pltpu.VMEM((2 * length_y, 2 * length_y), f32),
            pltpu.VMEM(layer, f32),
            pltpu.VMEM((length_z,) + layer, f32),
            pltpu.VMEM((2 * length_y, length_z), f32),
            dma((3,)), dma((2,)), dma((3,)), dma((3,)),
            dma((STEPS, 2)), dma((STEPS, 2)), dma((STEPS, 2)), dma((STEPS, 2)),
            dma((STEPS, 3, 2)), dma((STEPS, 3, 2)),
        ],
        compiler_params=pltpu.CompilerParams(
            collective_id=0, has_side_effects=True, vmem_limit_bytes=48 * 1024 * 1024
        ),
        name="impact",
    )(displacement, velocity, material, moduli, density, partner, active)


def solution(mesh):
    in_specs = (
        P("body", None, "gx", "yz", None),
        P("body", None, "gx", "yz", None),
        P("body", "gx", "yz", None),
        P(),
        P(),
        P(),
        P(),
    )
    out_specs = (P("body", None, "gx", "yz", None), P("body", None, "gx", "yz", None))
    return jax.shard_map(local, mesh=mesh, in_specs=in_specs, out_specs=out_specs, check_vma=False)
```

```python
import functools
import math

import jax
import jax.numpy as jnp
from jax import lax
from jax.experimental import pallas as pl
from jax.experimental.pallas import tpu as pltpu
from jax.sharding import PartitionSpec as P

STEPS = 4
STEP_TIME = 0.2
YIELD_SPAN = 0.5
PENALTY = 4.0
SOFT_WIDTH = 0.1
KERNEL_WIDTH = 1.5
LOG2E = 1.0 / math.log(2.0)
PLANE = math.sqrt(LOG2E / (2.0 * KERNEL_WIDTH * KERNEL_WIDTH))
GROUP = 8

MESH = pl.DeviceIdType.MESH
HIGHEST = lax.Precision.HIGHEST


def kernel(
    count_x, count_y, dims,
    disp, velo, mat_hbm, moduli_hbm, density_hbm, partner_hbm, active_hbm,
    out_d, out_v,
    D, V, M, E, SX, SY, SYL, SZ, SZB, C, PX,
    XH, YH, YS, MX, MY, MC, MYS, OT, CP, W, WTURN, ACT, WT, FY, FZ, FX,
    moduli, density, partner, active,
    load_sem, out_sem, m_send, m_recv, x_send, x_recv, y_send, y_recv, c_send, c_recv,
):
    length_x, length_y, length_z = dims
    last = length_x - 1
    body = lax.axis_index("body")
    gx = lax.axis_index("gx")
    yz = lax.axis_index("yz")
    has_lo = gx > 0
    has_hi = gx < count_x - 1
    has_dn = yz > 0
    has_up = yz < count_y - 1
    is_face = gx == count_x - 1
    cross = lax.rem(yz + 1 - 2 * body + count_y, count_y)
    other = 1 - body

    low = {"gx": gx - 1}
    high = {"gx": gx + 1}
    down = {"yz": yz - 1}
    up = {"yz": yz + 1}
    corner_up = {"gx": gx + 1, "yz": yz + 1}
    corner_dn = {"gx": gx - 1, "yz": yz - 1}
    same_peer = {"body": other}
    cross_peer = {"body": other, "yz": cross}

    row_id = lax.broadcasted_iota(jnp.int32, (length_y, length_z), 0)
    lane_id = lax.broadcasted_iota(jnp.int32, (length_y, length_z), 1)

    loads = [
        pltpu.make_async_copy(mat_hbm.at[0], M, load_sem.at[0]),
        pltpu.make_async_copy(disp.at[0], D.at[0], load_sem.at[1]),
        pltpu.make_async_copy(velo.at[0], V, load_sem.at[2]),
        pltpu.make_async_copy(moduli_hbm, moduli, load_sem.at[3]),
        pltpu.make_async_copy(density_hbm, density, load_sem.at[4]),
        pltpu.make_async_copy(partner_hbm, partner, load_sem.at[5]),
        pltpu.make_async_copy(active_hbm, active, load_sem.at[6]),
    ]
    for item in loads:
        item.start()

    barrier = pltpu.get_barrier_semaphore()

    def greet(condition, device):
        @pl.when(condition)
        def _():
            pl.semaphore_signal(barrier, inc=1, device_id=device, device_id_type=MESH)

    pairs = [
        (has_lo, low), (has_hi, high), (has_dn, down), (has_up, up),
        (has_hi & has_up, corner_up), (has_lo & has_dn, corner_dn),
        (is_face, same_peer), (is_face, cross_peer),
    ]
    for condition, device in pairs:
        greet(condition, device)
    pl.semaphore_wait(barrier, sum(condition.astype(jnp.int32) for condition, _ in pairs))

    def remote(source, target, send, recv, device):
        return pltpu.make_async_remote_copy(
            src_ref=source, dst_ref=target, send_sem=send, recv_sem=recv,
            device_id=device, device_id_type=MESH,
        )

    def x_up(s, source):
        return remote(source, XH.at[s, 0], x_send.at[s, 0], x_recv.at[s, 0], high)

    def x_down(s, source):
        return remote(source, XH.at[s, 1], x_send.at[s, 1], x_recv.at[s, 1], low)

    def y_up(s):
        return remote(YS.at[s, 0], YH.at[s, 0], y_send.at[s, 0], y_recv.at[s, 0], up)

    def y_down(s):
        return remote(YS.at[s, 1], YH.at[s, 1], y_send.at[s, 1], y_recv.at[s, 1], down)

    def c_same(s, c):
        return remote(OT.at[s, c], CP.at[s, c, 0], c_send.at[s, c, 0], c_recv.at[s, c, 0], same_peer)

    def c_cross(s, c):
        return remote(OT.at[s, c], CP.at[s, c, 1], c_send.at[s, c, 1], c_recv.at[s, c, 1], cross_peer)

    m_x = remote(mat_hbm.at[0, last], MX, m_send.at[0], m_recv.at[0], high)
    m_y = remote(MYS, MY, m_send.at[1], m_recv.at[1], up)
    m_c = remote(MYS.at[pl.ds(length_x - 8, 8)], MC, m_send.at[2], m_recv.at[2], corner_up)

    @pl.when(has_hi)
    def _():
        m_x.start()
        x_up(0, disp.at[0, :, last]).start()

    @pl.when(has_lo)
    def _():
        x_down(0, disp.at[0, :, 0]).start()

    half = length_z // 2
    low_lanes = lane_id < half

    def turn_face(s, c):
        own = D[s, c, last]
        turned = jnp.concatenate([own, own], axis=0).T
        OT[s, c] = jnp.where(low_lanes, turned[:half], turned[half:])

    def send_face(s, c):
        c_same(s, c).start()
        c_cross(s, c).start()

    @pl.when(jnp.logical_not(has_lo))
    def _():
        XH[:, 0] = jnp.zeros((STEPS, 3, length_y, length_z), jnp.float32)

    @pl.when(jnp.logical_not(has_hi))
    def _():
        XH[:, 1] = jnp.zeros((STEPS, 3, length_y, length_z), jnp.float32)

    @pl.when(jnp.logical_not(has_dn))
    def _():
        YH[:, 0] = jnp.zeros((STEPS, 3, length_x, length_z), jnp.float32)
        MY[...] = jnp.zeros((length_x, length_z), jnp.int32)

    @pl.when(jnp.logical_not(has_up))
    def _():
        YH[:, 1] = jnp.zeros((STEPS, 3, length_x, length_z), jnp.float32)

    @pl.when(jnp.logical_not(has_lo))
    def _():
        MX[...] = jnp.zeros((length_y, length_z), jnp.int32)

    @pl.when(jnp.logical_not(has_lo & has_dn))
    def _():
        MC[...] = jnp.zeros((8, length_z), jnp.int32)

    loads[0].wait()

    @pl.loop(0, length_x)
    def _(i):
        MYS[pl.ds(i, 1)] = M[i, pl.ds(length_y - 1, 1)]

    @pl.when(has_up)
    def _():
        m_y.start()

    @pl.when(has_hi & has_up)
    def _():
        m_c.start()

    loads[1].wait()

    @pl.loop(0, length_x)
    def _(i):
        for c in range(3):
            doubled = D[0, c, i] * (1.0 / YIELD_SPAN)
            D[0, c, i] = doubled
            YS[0, 0, c, pl.ds(i, 1)] = doubled[length_y - 1 :]
            YS[0, 1, c, pl.ds(i, 1)] = doubled[:1]

    @pl.when(is_face)
    def _():
        for c in (1, 2, 0):
            turn_face(0, c)
        for c in (1, 2, 0):
            send_face(0, c)

    @pl.when(has_up)
    def _():
        y_up(0).start()

    @pl.when(has_dn)
    def _():
        y_down(0).start()

    for item in loads[3:]:
        item.wait()

    def lookup(kinds, table):
        result = jnp.full(kinds.shape, table[0], jnp.float32)
        for kind in range(1, 8):
            result = jnp.where(kinds == kind, table[kind], result)
        return result

    inner_lane = lane_id < length_z - 1
    own_edge = inner_lane & jnp.logical_or(has_up, row_id < length_y - 1)

    @pl.loop(0, length_x)
    def _(i):
        kinds = M[i]
        keep = own_edge & (jnp.logical_or(has_hi, i < last))
        E[i + 1, pl.ds(8, length_y)] = jnp.where(keep, lookup(kinds, moduli), 0.0)
        C[i] = (STEP_TIME * STEP_TIME / YIELD_SPAN) / lookup(kinds, density)

    @pl.when(is_face)
    def _():
        base = yz * length_y
        side_base = cross * length_y
        lanes = 2 * length_y
        out_lane = lax.broadcasted_iota(jnp.int32, (1, lanes), 1)

        @pl.when(body == 0)
        def _():
            pool_lane = lax.broadcasted_iota(jnp.int32, (1, 2 * lanes), 1)

            def fill(row, total):
                upper = jnp.where(row >= length_y, 1, 0)
                own = base + row - upper * length_y
                wanted = partner[own]
                near = (wanted >= base) & (wanted < base + length_y)
                column = jnp.where(near, wanted - base, wanted - side_base + lanes) + upper * length_y
                WTURN[pl.ds(row, 1)] = jnp.where(pool_lane == column, 1.0, 0.0)
                return total + jnp.where(out_lane == row, active[own].astype(jnp.float32), 0.0)

            live = lax.fori_loop(0, lanes, fill, jnp.zeros((1, lanes), jnp.float32))
            ACT[...] = live * (-PENALTY * SOFT_WIDTH)
            W[...] = WTURN[...].T

        @pl.when(body == 1)
        def _():
            def fill(row, total):
                upper = jnp.where(lax.rem(row, lanes) >= length_y, 1, 0)
                spot = lax.rem(row, length_y)
                own = jnp.where(row < lanes, base, side_base) + spot
                wanted = partner[own] - base
                match = (out_lane == wanted + upper * length_y) & (
                    (out_lane >= upper * length_y) & (out_lane < (upper + 1) * length_y)
                )
                line = jnp.where(match, 1.0, 0.0)
                W[pl.ds(row, 1)] = line
                return total + line * active[own].astype(jnp.float32)

            live = lax.fori_loop(0, 2 * lanes, fill, jnp.zeros((1, lanes), jnp.float32))
            ACT[...] = live * (-PENALTY * SOFT_WIDTH)

    @pl.when(has_lo)
    def _():
        m_x.wait_recv()

    @pl.when(has_dn)
    def _():
        m_y.wait_recv()

    @pl.when(has_lo & has_dn)
    def _():
        m_c.wait_recv()

    E[0, pl.ds(8, length_y)] = jnp.where(own_edge & has_lo, lookup(MX[...], moduli), 0.0)
    row_lane = lax.broadcasted_iota(jnp.int32, (length_x, length_z), 1) < length_z - 1
    row_pos = lax.broadcasted_iota(jnp.int32, (length_x, length_z), 0)
    side = jnp.where(
        row_lane & has_dn & jnp.logical_or(has_hi, row_pos < last), lookup(MY[...], moduli), 0.0
    )
    SYL[...] = side
    E[0, pl.ds(7, 1)] = jnp.where(
        inner_lane[:1] & has_lo & has_dn, lookup(MC[pl.ds(7, 1)], moduli), 0.0
    )

    @pl.loop(0, length_x)
    def _(i):
        E[i + 1, pl.ds(7, 1)] = SYL[pl.ds(i, 1)]

    def with_left(value):
        return value + pltpu.roll(value, 1, 1)

    quarter = 0.25 * YIELD_SPAN

    @pl.loop(0, length_x + 1)
    def _(i):
        whole = E[i]
        here = whole[8:]
        behind = pltpu.roll(whole, 1, 0)[8:]
        SX[i] = quarter * with_left(here + behind)

        @pl.when(i > 0)
        def _():
            under = E[i - 1]
            both = whole + under
            SY[i - 1] = quarter * with_left(both[8:])
            edge = quarter * (both + pltpu.roll(both, 1, 0))[8:]
            SZ[i - 1] = edge
            SZB[i - 1] = pltpu.roll(edge, 1, 1)
            SYL[pl.ds(i - 1, 1)] = quarter * with_left(both[7:8])

    loads[2].wait()

    @pl.loop(0, length_x)
    def _(i):
        for c in range(3):
            V[c, i] = V[c, i] * (STEP_TIME / YIELD_SPAN)

    def node_update(s, c, x, here, pull_x, pull_x_below, extra=None):
        ahead = pltpu.roll(here, length_y - 1, 0)
        ahead = jnp.where(row_id == length_y - 1, YH[s, 1, c, pl.ds(x, 1)], ahead)
        pull_y = SY[x] * jnp.tanh(ahead - here)
        first = SYL[pl.ds(x, 1)] * jnp.tanh(here[:1] - YH[s, 0, c, pl.ds(x, 1)])
        below = jnp.where(row_id == 0, first, pltpu.roll(pull_y, 1, 0))
        pull_z = SZ[x] * jnp.tanh(pltpu.roll(here, length_z - 1, 1) - here)
        pull_z_below = SZB[x] * jnp.tanh(here - pltpu.roll(here, 1, 1))
        force = (pull_x - pull_x_below) + (pull_y - below) + (pull_z - pull_z_below)
        if extra is not None:
            force = force + extra
        speed = V[c, x] + C[x] * force
        V[c, x] = speed
        moved = here + speed
        D[s + 1, c, x] = moved
        YS[s + 1, 0, c, pl.ds(x, 1)] = moved[length_y - 1 :]
        YS[s + 1, 1, c, pl.ds(x, 1)] = moved[:1]

    def raw_scale(s):
        return jnp.where(s == 0, 1.0 / YIELD_SPAN, 1.0)

    def first_layer(s, c):
        here = D[s, c, 0]
        pull_below = SX[0] * jnp.tanh(here - XH[s, 0, c] * raw_scale(s))
        pull_x = SX[1] * jnp.tanh(D[s, c, 1] - here)
        PX[c] = pull_x
        node_update(s, c, 0, here, pull_x, pull_below)

    def last_layer(s, c, extra=None):
        here = D[s, c, last]
        pull_below = SX[last] * jnp.tanh(here - D[s, c, last - 1])
        pull_x = SX[last + 1] * jnp.tanh(XH[s, 1, c] * raw_scale(s) - here)
        node_update(s, c, last, here, pull_x, pull_below, extra)

    def matched(s, c):
        pool = jnp.concatenate([CP[s, c, 0], CP[s, c, 1]], axis=1)
        high = pool.astype(jnp.bfloat16)
        rest = pool - high.astype(jnp.float32)
        middle = rest.astype(jnp.bfloat16)
        tail = (rest - middle.astype(jnp.float32)).astype(jnp.bfloat16)
        pick = W[...].astype(jnp.bfloat16)
        parts = [
            jnp.dot(part, pick, preferred_element_type=jnp.float32) for part in (high, middle, tail)
        ]
        return (parts[0] + parts[1]) + parts[2]

    def spread(ref, lower, upper):
        ref[pl.ds(0, half)] = lower
        ref[pl.ds(half, half)] = upper
        ref[pl.ds(2 * half, half)] = lower

    half_rows = row_id[:half]
    half_lanes = lane_id[:half]
    place = (half_rows + jnp.where(half_lanes < half, 0, half)).astype(jnp.float32)
    place_other = (half_rows + jnp.where(half_lanes < half, half, 0)).astype(jnp.float32)
    depth = LOG2E / SOFT_WIDTH * YIELD_SPAN

    def weights(s):
        far_y = matched(s, 1) * (PLANE * YIELD_SPAN)
        far_z = matched(s, 2) * YIELD_SPAN
        spread(FY, far_y, pltpu.roll(far_y, half, 1))
        spread(FZ, (far_z + place) * PLANE, (pltpu.roll(far_z, half, 1) + place_other) * PLANE)
        own_y = OT[s, 1] * (PLANE * YIELD_SPAN)
        own_z = (OT[s, 2] * YIELD_SPAN + place) * PLANE

        @pl.loop(0, length_z // GROUP)
        def _(block):
            for k in range(GROUP):
                turn = block * GROUP + k
                along_y = own_y - FY[pl.ds(turn, half)]
                along_z = own_z - FZ[pl.ds(turn, half)]
                WT[turn] = jnp.exp2((0.0 - along_y * along_y) - along_z * along_z)

    def contact(s):
        far_x = matched(s, 0) * depth
        spread(FX, far_x, pltpu.roll(far_x, half, 1))
        own_x = OT[s, 0] * depth

        def group(block, total):
            for k in range(GROUP):
                turn = block * GROUP + k
                squeeze = own_x + FX[pl.ds(turn, half)]
                hard = jnp.maximum(squeeze, 0.0)
                soft = jnp.log(1.0 + jnp.exp2(squeeze - (hard + hard)))
                total = total + WT[turn] * (hard * math.log(2.0) + soft)
            return total

        total = lax.fori_loop(
            0, length_z // GROUP, group, jnp.zeros((half, length_z), jnp.float32)
        )
        total = total * ACT[...]
        turned = jnp.concatenate([total, total], axis=0).T
        return jnp.where(low_lanes, turned[:length_y], turned[length_y:])

    def step(s, carry):
        more = s + 1 < STEPS

        @pl.when(is_face)
        def _():
            for c in (1, 2):
                c_same(s, c).wait_recv()
                c_cross(s, c).wait_recv()
            weights(s)

        @pl.when(has_dn)
        def _():
            y_up(s).wait_recv()

        @pl.when(has_up)
        def _():
            y_down(s).wait_recv()

        @pl.when(has_hi)
        def _():
            x_down(s, D.at[s, :, 0]).wait_recv()
            for c in range(3):
                last_layer(s, c)

            @pl.when(more)
            def _():
                x_up(s + 1, D.at[s + 1, :, last]).start()

        @pl.when(is_face)
        def _():
            for c in (1, 2):
                last_layer(s, c)
                turn_face(s + 1, c)

            @pl.when(more)
            def _():
                for c in (1, 2):
                    send_face(s + 1, c)

        @pl.when(has_lo)
        def _():
            x_up(s, D.at[s, :, last]).wait_recv()

        for c in range(3):
            first_layer(s, c)

        @pl.when(more & has_lo)
        def _():
            x_down(s + 1, D.at[s + 1, :, 0]).start()

        @pl.loop(0, (last - 1) // 2)
        def _(pair):
            for offset in range(2):
                x = 2 * pair + 1 + offset
                for c in range(3):
                    here = D[s, c, x]
                    pull_x = SX[x + 1] * jnp.tanh(D[s, c, x + 1] - here)
                    below = PX[c]
                    PX[c] = pull_x
                    node_update(s, c, x, here, pull_x, below)

        @pl.when(is_face)
        def _():
            c_same(s, 0).wait_recv()
            c_cross(s, 0).wait_recv()
            last_layer(s, 0, contact(s))

            @pl.when(more)
            def _():
                turn_face(s + 1, 0)
                send_face(s + 1, 0)

        @pl.when(more & has_up)
        def _():
            y_up(s + 1).start()

        @pl.when(more & has_dn)
        def _():
            y_down(s + 1).start()

        return carry

    lax.fori_loop(0, STEPS, step, 0)

    stores = [
        pltpu.make_async_copy(D.at[STEPS], out_d.at[0], out_sem.at[0]),
        pltpu.make_async_copy(V, out_v.at[0], out_sem.at[1]),
    ]
    for item in stores:
        item.start()

    @pl.when(has_hi)
    def _():
        m_x.wait_send()

    @pl.when(has_up)
    def _():
        m_y.wait_send()

    @pl.when(has_hi & has_up)
    def _():
        m_c.wait_send()

    def drain(s, carry):
        @pl.when(has_hi)
        def _():
            x_up(s, D.at[s, :, last]).wait_send()

        @pl.when(has_lo)
        def _():
            x_down(s, D.at[s, :, 0]).wait_send()

        @pl.when(has_up)
        def _():
            y_up(s).wait_send()

        @pl.when(has_dn)
        def _():
            y_down(s).wait_send()

        @pl.when(is_face)
        def _():
            for c in range(3):
                c_same(s, c).wait_send()
                c_cross(s, c).wait_send()

        return carry

    lax.fori_loop(0, STEPS, drain, 0)
    for item in stores:
        item.wait()


def local(displacement, velocity, material, moduli, density, partner, active):
    length_x, length_y, length_z = displacement.shape[2:]
    count_x = lax.axis_size("gx")
    count_y = lax.axis_size("yz")
    f32 = jnp.float32
    i32 = jnp.int32
    layer = (length_y, length_z)
    solid = (length_x,) + layer
    anywhere = pl.BlockSpec(memory_space=pl.ANY)
    far_memory = pl.BlockSpec(memory_space=pltpu.HBM)
    dma = pltpu.SemaphoreType.DMA
    half = length_z // 2
    scaled_d, scaled_v = pl.pallas_call(
        functools.partial(kernel, count_x, count_y, (length_x, length_y, length_z)),
        out_shape=(
            jax.ShapeDtypeStruct(displacement.shape, f32),
            jax.ShapeDtypeStruct(velocity.shape, f32),
        ),
        in_specs=[far_memory] * 7,
        out_specs=(anywhere, anywhere),
        scratch_shapes=[
            pltpu.VMEM((STEPS + 1, 3) + solid, f32),
            pltpu.VMEM((3,) + solid, f32),
            pltpu.VMEM(solid, i32),
            pltpu.VMEM((length_x + 1, length_y + 8, length_z), f32),
            pltpu.VMEM((length_x + 1,) + layer, f32),
            pltpu.VMEM(solid, f32),
            pltpu.VMEM((length_x, length_z), f32),
            pltpu.VMEM(solid, f32),
            pltpu.VMEM(solid, f32),
            pltpu.VMEM(solid, f32),
            pltpu.VMEM((3,) + layer, f32),
            pltpu.VMEM((STEPS, 2, 3) + layer, f32),
            pltpu.VMEM((STEPS, 2, 3, length_x, length_z), f32),
            pltpu.VMEM((STEPS + 1, 2, 3, length_x, length_z), f32),
            pltpu.VMEM(layer, i32),
            pltpu.VMEM((length_x, length_z), i32),
            pltpu.VMEM((8, length_z), i32),
            pltpu.VMEM((length_x, length_z), i32),
            pltpu.VMEM((STEPS + 1, 3, half, 2 * length_y), f32),
            pltpu.VMEM((STEPS, 3, 2, half, 2 * length_y), f32),
            pltpu.VMEM((4 * length_y, 2 * length_y), f32),
            pltpu.VMEM((2 * length_y, 4 * length_y), f32),
            pltpu.VMEM((1, 2 * length_y), f32),
            pltpu.VMEM((length_z, half, 2 * length_y), f32),
            pltpu.VMEM((3 * half, 2 * length_y), f32),
            pltpu.VMEM((3 * half, 2 * length_y), f32),
            pltpu.VMEM((3 * half, 2 * length_y), f32),
            pltpu.SMEM(moduli.shape, f32),
            pltpu.SMEM(density.shape, f32),
            pltpu.SMEM(partner.shape, i32),
            pltpu.SMEM(active.shape, i32),
            dma((7,)), dma((2,)), dma((3,)), dma((3,)),
            dma((STEPS, 2)), dma((STEPS, 2)), dma((STEPS, 2)), dma((STEPS, 2)),
            dma((STEPS, 3, 2)), dma((STEPS, 3, 2)),
        ],
        compiler_params=pltpu.CompilerParams(
            collective_id=0, has_side_effects=True, vmem_limit_bytes=48 * 1024 * 1024
        ),
        name="impact",
    )(*[
        pltpu.with_memory_space_constraint(item, pltpu.HBM)
        for item in (displacement, velocity, material, moduli, density, partner, active)
    ])
    return scaled_d * YIELD_SPAN, scaled_v * (YIELD_SPAN / STEP_TIME)


def solution(mesh):
    in_specs = (
        P("body", None, "gx", "yz", None),
        P("body", None, "gx", "yz", None),
        P("body", "gx", "yz", None),
        P(),
        P(),
        P(),
        P(),
    )
    out_specs = (P("body", None, "gx", "yz", None), P("body", None, "gx", "yz", None))
    return jax.shard_map(local, mesh=mesh, in_specs=in_specs, out_specs=out_specs, check_vma=False)
```

```python
import functools
import math

import jax
import jax.numpy as jnp
from jax import lax
from jax.experimental import pallas as pl
from jax.experimental.pallas import tpu as pltpu
from jax.sharding import PartitionSpec as P

STEPS = 4
STEP_TIME = 0.2
YIELD_SPAN = 0.5
PENALTY = 4.0
SOFT_WIDTH = 0.1
KERNEL_WIDTH = 1.5
LOG2E = 1.0 / math.log(2.0)
PLANE = math.sqrt(LOG2E / (2.0 * KERNEL_WIDTH * KERNEL_WIDTH))
GROUP = 16

MESH = pl.DeviceIdType.MESH
HIGHEST = lax.Precision.HIGHEST


def kernel(
    count_x, count_y, dims,
    disp, velo, mat_hbm, moduli_hbm, density_hbm, partner_hbm, active_hbm,
    out_d, out_v,
    D, V, M, E, SX, SY, SYL, SZ, SZB, C, PX,
    XH, YH, YS, YLH, YLS, MX, MY, MC, MYS, CS, CP, GIVE, TAKE, ACT, WT, FY, FZ, FX,
    partner, active, moduli, density,
    load_sem, out_sem, m_send, m_recv, x_send, x_recv, y_send, y_recv, l_send, l_recv, c_send, c_recv,
):
    length_x, length_y, length_z = dims
    last = length_x - 1
    body = lax.axis_index("body")
    gx = lax.axis_index("gx")
    yz = lax.axis_index("yz")
    has_lo = gx > 0
    has_hi = gx < count_x - 1
    has_dn = yz > 0
    has_up = yz < count_y - 1
    is_face = gx == count_x - 1
    cross = lax.rem(yz + 1 - 2 * body + count_y, count_y)
    other = 1 - body

    quota = length_y // 2
    low = {"gx": gx - 1}
    high = {"gx": gx + 1}
    down = {"yz": yz - 1}
    up = {"yz": yz + 1}
    corner_up = {"gx": gx + 1, "yz": yz + 1}
    corner_dn = {"gx": gx - 1, "yz": yz - 1}
    same_peer = {"body": other}
    cross_peer = {"body": other, "yz": cross}

    row_id = lax.broadcasted_iota(jnp.int32, (length_y, length_z), 0)
    lane_id = lax.broadcasted_iota(jnp.int32, (length_y, length_z), 1)

    loads = [
        pltpu.make_async_copy(mat_hbm.at[0], M, load_sem.at[0]),
        pltpu.make_async_copy(disp.at[0], D.at[0], load_sem.at[1]),
        pltpu.make_async_copy(velo.at[0], V, load_sem.at[2]),
        pltpu.make_async_copy(moduli_hbm, moduli, load_sem.at[3]),
        pltpu.make_async_copy(density_hbm, density, load_sem.at[4]),
        pltpu.make_async_copy(partner_hbm, partner, load_sem.at[5]),
        pltpu.make_async_copy(active_hbm, active, load_sem.at[6]),
    ]
    for item in loads:
        item.start()

    barrier = pltpu.get_barrier_semaphore()

    def greet(condition, device):
        @pl.when(condition)
        def _():
            pl.semaphore_signal(barrier, inc=1, device_id=device, device_id_type=MESH)

    pairs = [
        (has_lo, low), (has_hi, high), (has_dn, down), (has_up, up),
        (has_hi & has_up, corner_up), (has_lo & has_dn, corner_dn),
        (is_face, same_peer), (is_face, cross_peer),
    ]
    for condition, device in pairs:
        greet(condition, device)
    pl.semaphore_wait(barrier, sum(condition.astype(jnp.int32) for condition, _ in pairs))

    def remote(source, target, send, recv, device):
        return pltpu.make_async_remote_copy(
            src_ref=source, dst_ref=target, send_sem=send, recv_sem=recv,
            device_id=device, device_id_type=MESH,
        )

    def x_up(s, c, source):
        return remote(source, XH.at[s, 0, c], x_send.at[s, 0, c], x_recv.at[s, 0, c], high)

    def x_down(s, c, source):
        return remote(source, XH.at[s, 1, c], x_send.at[s, 1, c], x_recv.at[s, 1, c], low)

    def late_up(s):
        return remote(YLS.at[s, 0], YLH.at[s, 0], l_send.at[s, 0], l_recv.at[s, 0], up)

    def late_down(s):
        return remote(YLS.at[s, 1], YLH.at[s, 1], l_send.at[s, 1], l_recv.at[s, 1], down)

    def y_up(s):
        return remote(YS.at[s, 0], YH.at[s, 0], y_send.at[s, 0], y_recv.at[s, 0], up)

    def y_down(s):
        return remote(YS.at[s, 1], YH.at[s, 1], y_send.at[s, 1], y_recv.at[s, 1], down)

    def c_same(s, c):
        return remote(
            CS.at[s, c, pl.ds(0, quota)], CP.at[s, c, pl.ds(0, quota)],
            c_send.at[s, c, 0], c_recv.at[s, c, 0], same_peer,
        )

    def c_cross(s, c):
        return remote(
            CS.at[s, c, pl.ds(quota, quota)], CP.at[s, c, pl.ds(quota, quota)],
            c_send.at[s, c, 1], c_recv.at[s, c, 1], cross_peer,
        )

    m_x = remote(mat_hbm.at[0, last], MX, m_send.at[0], m_recv.at[0], high)
    m_y = remote(MYS, MY, m_send.at[1], m_recv.at[1], up)
    m_c = remote(MYS.at[pl.ds(length_x - 8, 8)], MC, m_send.at[2], m_recv.at[2], corner_up)

    @pl.when(has_hi)
    def _():
        m_x.start()
        for c in range(3):
            x_up(0, c, disp.at[0, c, last]).start()

    @pl.when(has_lo)
    def _():
        for c in range(3):
            x_down(0, c, disp.at[0, c, 0]).start()

    half = length_z // 2
    low_lanes = lane_id < half

    def exact_pick(choice, value):
        high_part = value.astype(jnp.bfloat16)
        rest = value - high_part.astype(jnp.float32)
        middle = rest.astype(jnp.bfloat16)
        tail = (rest - middle.astype(jnp.float32)).astype(jnp.bfloat16)
        upper_parts = jnp.concatenate([high_part, middle], axis=0)
        lower_parts = jnp.concatenate([tail, jnp.zeros_like(tail)], axis=0)
        return jnp.dot(choice, upper_parts, preferred_element_type=jnp.float32) + jnp.dot(
            choice, lower_parts, preferred_element_type=jnp.float32
        )

    def turned_pair(value):
        turned = jnp.concatenate([value, value], axis=0).T
        return turned[:half], turned[half:]

    def own_face(s, c):
        lower, upper = turned_pair(D[s, c, last])
        return jnp.where(low_lanes, lower, upper)

    def pack_face(s, c):
        CS[s, c] = exact_pick(GIVE[...], D[s, c, last])

    def send_face(s, c):
        c_same(s, c).start()
        c_cross(s, c).start()

    @pl.when(jnp.logical_not(has_lo))
    def _():
        XH[:, 0] = jnp.zeros((STEPS, 3, length_y, length_z), jnp.float32)

    @pl.when(jnp.logical_not(has_hi))
    def _():
        XH[:, 1] = jnp.zeros((STEPS, 3, length_y, length_z), jnp.float32)

    @pl.when(jnp.logical_not(has_dn))
    def _():
        YH[:, 0] = jnp.zeros((STEPS, 3, length_x, length_z), jnp.float32)
        YLH[:, 0] = jnp.zeros((STEPS, 8, length_z), jnp.float32)
        MY[...] = jnp.zeros((length_x, length_z), jnp.int32)

    @pl.when(jnp.logical_not(has_up))
    def _():
        YH[:, 1] = jnp.zeros((STEPS, 3, length_x, length_z), jnp.float32)
        YLH[:, 1] = jnp.zeros((STEPS, 8, length_z), jnp.float32)

    @pl.when(jnp.logical_not(has_lo))
    def _():
        MX[...] = jnp.zeros((length_y, length_z), jnp.int32)

    @pl.when(jnp.logical_not(has_lo & has_dn))
    def _():
        MC[...] = jnp.zeros((8, length_z), jnp.int32)

    loads[0].wait()

    @pl.loop(0, length_x)
    def _(i):
        MYS[pl.ds(i, 1)] = M[i, pl.ds(length_y - 1, 1)]

    @pl.when(has_up)
    def _():
        m_y.start()

    @pl.when(has_hi & has_up)
    def _():
        m_c.start()

    for item in loads[3:]:
        item.wait()

    @pl.when(is_face)
    def _():
        base = yz * length_y
        size = (2 * length_y, 2 * length_y)
        rows = lax.broadcasted_iota(jnp.int32, size, 0)
        lanes = lax.broadcasted_iota(jnp.int32, size, 1)

        def publish(mate_col, mate_row, live):
            near_col = (mate_col >= base) & (mate_col < base + length_y)
            near_row = (mate_row >= base) & (mate_row < base + length_y)
            shift_col = jnp.where(near_col, 0.0, 1.0)
            shift_row = jnp.where(near_row, 0.0, 1.0)
            alike = shift_col == shift_row
            before = jnp.where(alike & (mate_row < mate_col) & (lanes < length_y), 1.0, 0.0)
            spot = jnp.sum(before, axis=1, keepdims=True) + quota * shift_col
            name = lanes.astype(jnp.float32)
            TAKE[...] = jnp.where(
                (name == spot) | (name == spot + float(length_y)), 1.0, 0.0
            )[:length_y].astype(jnp.bfloat16)
            earlier = jnp.where(alike & (rows < lanes) & (rows < length_y), 1.0, 0.0)
            slot = jnp.sum(earlier, axis=0, keepdims=True) + quota * shift_row
            single = jnp.where(rows.astype(jnp.float32) == slot, 1.0, 0.0)
            GIVE[...] = jnp.where(lanes < length_y, single, pltpu.roll(single, length_y, 1))[
                :length_y
            ].astype(jnp.bfloat16)
            ACT[...] = live[:length_y] * (-PENALTY * SOFT_WIDTH)

        @pl.when(body == 0)
        def _():
            def own_block(table):
                line = jnp.where(yz < 2, table[pl.ds(0, 1)], table[pl.ds(1, 1)])
                moved = jnp.where(lax.rem(yz, 2) == 0, line, pltpu.roll(line, half, 1))
                return jnp.broadcast_to(moved.astype(jnp.float32), size)

            across = own_block(partner)
            publish(across.T.astype(jnp.int32), across.astype(jnp.int32), own_block(active).T)

        @pl.when(body == 1)
        def _():
            mate = jnp.zeros((2 * length_y, 1), jnp.float32)
            live = jnp.zeros((2 * length_y, 1), jnp.float32)
            for part in range(2):
                hit = jnp.where(partner[pl.ds(part, 1)] == rows + base, 1.0, 0.0)
                name = (lanes + part * length_z).astype(jnp.float32)
                mate = mate + jnp.sum(hit * name, axis=1, keepdims=True)
                live = live + jnp.sum(
                    hit * active[pl.ds(part, 1)].astype(jnp.float32), axis=1, keepdims=True
                )
            down_rows = jnp.broadcast_to(mate, size)
            publish(
                down_rows.astype(jnp.int32), down_rows.T.astype(jnp.int32),
                jnp.broadcast_to(live, size),
            )

    loads[1].wait()

    @pl.loop(0, length_x)
    def _(i):
        for c in range(3):
            doubled = D[0, c, i] * (1.0 / YIELD_SPAN)
            D[0, c, i] = doubled
            YS[0, 0, c, pl.ds(i, 1)] = doubled[length_y - 1 :]
            YS[0, 1, c, pl.ds(i, 1)] = doubled[:1]

    def send_late(s):
        @pl.when(has_up)
        def _():
            late_up(s).start()

        @pl.when(has_dn)
        def _():
            late_down(s).start()

    @pl.when(is_face)
    def _():
        YLS[0, 0, pl.ds(0, 1)] = D[0, 0, last, pl.ds(length_y - 1, 1)]
        YLS[0, 1, pl.ds(0, 1)] = D[0, 0, last, pl.ds(0, 1)]
        send_late(0)
        for c in (1, 2, 0):
            pack_face(0, c)
        for c in (1, 2, 0):
            send_face(0, c)

    @pl.when(has_up)
    def _():
        y_up(0).start()

    @pl.when(has_dn)
    def _():
        y_down(0).start()

    def lookup(kinds, table):
        result = jnp.full(kinds.shape, table[0], jnp.float32)
        for kind in range(1, 8):
            result = jnp.where(kinds == kind, table[kind], result)
        return result

    inner_lane = lane_id < length_z - 1
    own_edge = inner_lane & jnp.logical_or(has_up, row_id < length_y - 1)

    @pl.loop(0, length_x)
    def _(i):
        kinds = M[i]
        keep = own_edge & (jnp.logical_or(has_hi, i < last))
        E[i + 1, pl.ds(8, length_y)] = jnp.where(keep, lookup(kinds, moduli), 0.0)
        C[i] = (STEP_TIME * STEP_TIME / YIELD_SPAN) / lookup(kinds, density)

    @pl.when(has_lo)
    def _():
        m_x.wait_recv()

    @pl.when(has_dn)
    def _():
        m_y.wait_recv()

    @pl.when(has_lo & has_dn)
    def _():
        m_c.wait_recv()

    E[0, pl.ds(8, length_y)] = jnp.where(own_edge & has_lo, lookup(MX[...], moduli), 0.0)
    row_lane = lax.broadcasted_iota(jnp.int32, (length_x, length_z), 1) < length_z - 1
    row_pos = lax.broadcasted_iota(jnp.int32, (length_x, length_z), 0)
    side = jnp.where(
        row_lane & has_dn & jnp.logical_or(has_hi, row_pos < last), lookup(MY[...], moduli), 0.0
    )
    SYL[...] = side
    E[0, pl.ds(7, 1)] = jnp.where(
        inner_lane[:1] & has_lo & has_dn, lookup(MC[pl.ds(7, 1)], moduli), 0.0
    )

    @pl.loop(0, length_x)
    def _(i):
        E[i + 1, pl.ds(7, 1)] = SYL[pl.ds(i, 1)]

    def with_left(value):
        return value + pltpu.roll(value, 1, 1)

    quarter = 0.25 * YIELD_SPAN

    @pl.loop(0, length_x + 1)
    def _(i):
        whole = E[i]
        here = whole[8:]
        behind = pltpu.roll(whole, 1, 0)[8:]
        SX[i] = quarter * with_left(here + behind)

        @pl.when(i > 0)
        def _():
            under = E[i - 1]
            both = whole + under
            SY[i - 1] = quarter * with_left(both[8:])
            edge = quarter * (both + pltpu.roll(both, 1, 0))[8:]
            SZ[i - 1] = edge
            SZB[i - 1] = pltpu.roll(edge, 1, 1)
            SYL[pl.ds(i - 1, 1)] = quarter * with_left(both[7:8])

    loads[2].wait()

    @pl.loop(0, length_x)
    def _(i):
        for c in range(3):
            V[c, i] = V[c, i] * (STEP_TIME / YIELD_SPAN)

    def node_update(s, c, x, here, pull_x, pull_x_below, push=None):
        if push is None:
            row_up, row_down = YH[s, 1, c, pl.ds(x, 1)], YH[s, 0, c, pl.ds(x, 1)]
        else:
            row_up, row_down = YLH[s, 1, pl.ds(0, 1)], YLH[s, 0, pl.ds(0, 1)]
        ahead = pltpu.roll(here, length_y - 1, 0)
        ahead = jnp.where(row_id == length_y - 1, row_up, ahead)
        pull_y = SY[x] * jnp.tanh(ahead - here)
        first = SYL[pl.ds(x, 1)] * jnp.tanh(here[:1] - row_down)
        below = jnp.where(row_id == 0, first, pltpu.roll(pull_y, 1, 0))
        pull_z = SZ[x] * jnp.tanh(pltpu.roll(here, length_z - 1, 1) - here)
        pull_z_below = SZB[x] * jnp.tanh(here - pltpu.roll(here, 1, 1))
        force = (pull_x - pull_x_below) + (pull_y - below) + (pull_z - pull_z_below)
        if push is not None:
            force = force + push
        speed = V[c, x] + C[x] * force
        V[c, x] = speed
        moved = here + speed
        D[s + 1, c, x] = moved
        if push is None:
            YS[s + 1, 0, c, pl.ds(x, 1)] = moved[length_y - 1 :]
            YS[s + 1, 1, c, pl.ds(x, 1)] = moved[:1]
        else:
            YLS[s + 1, 0, pl.ds(0, 1)] = moved[length_y - 1 :]
            YLS[s + 1, 1, pl.ds(0, 1)] = moved[:1]

    def raw_scale(s):
        return jnp.where(s == 0, 1.0 / YIELD_SPAN, 1.0)

    def first_layer(s, c):
        here = D[s, c, 0]
        pull_below = SX[0] * jnp.tanh(here - XH[s, 0, c] * raw_scale(s))
        pull_x = SX[1] * jnp.tanh(D[s, c, 1] - here)
        PX[c] = pull_x
        node_update(s, c, 0, here, pull_x, pull_below)

    def last_layer(s, c, push=None):
        here = D[s, c, last]
        pull_below = SX[last] * jnp.tanh(here - D[s, c, last - 1])
        pull_x = SX[last + 1] * jnp.tanh(XH[s, 1, c] * raw_scale(s) - here)
        node_update(s, c, last, here, pull_x, pull_below, push)

    def matched(s, c):
        return turned_pair(exact_pick(TAKE[...], CP[s, c]))

    def spread(ref, lower, upper):
        near = jnp.where(low_lanes, lower, upper)
        other_half = jnp.where(low_lanes, upper, lower)
        ref[pl.ds(0, half)] = near
        ref[pl.ds(half, half)] = other_half
        ref[pl.ds(2 * half, half)] = near

    row_place = row_id.astype(jnp.float32)
    place = row_place + jnp.where(low_lanes, 0.0, float(half))
    depth = LOG2E / SOFT_WIDTH * YIELD_SPAN

    def weights(s):
        lower, upper = matched(s, 1)
        spread(FY, lower * (PLANE * YIELD_SPAN), upper * (PLANE * YIELD_SPAN))
        lower, upper = matched(s, 2)
        spread(
            FZ,
            (lower * YIELD_SPAN + row_place) * PLANE,
            (upper * YIELD_SPAN + (row_place + float(half))) * PLANE,
        )
        own_y = own_face(s, 1) * (PLANE * YIELD_SPAN)
        own_z = (own_face(s, 2) * YIELD_SPAN + place) * PLANE

        @pl.loop(0, length_z // GROUP)
        def _(block):
            for k in range(GROUP):
                turn = block * GROUP + k
                along_y = own_y - FY[pl.ds(turn, half)]
                along_z = own_z - FZ[pl.ds(turn, half)]
                WT[turn] = jnp.exp2((0.0 - along_y * along_y) - along_z * along_z)

    def contact(s, own_x):
        lower, upper = matched(s, 0)
        spread(FX, lower * depth, upper * depth)

        def group(block, total):
            for k in range(GROUP):
                turn = block * GROUP + k
                squeeze = own_x + FX[pl.ds(turn, half)]
                soft = jnp.log(1.0 + jnp.exp2(jnp.minimum(squeeze, 64.0)))
                total = total + WT[turn] * jnp.maximum(soft, squeeze * math.log(2.0))
            return total

        total = lax.fori_loop(
            0, length_z // GROUP, group, jnp.zeros((half, length_z), jnp.float32)
        )
        lower, upper = turned_pair(total)
        return jnp.where(low_lanes, lower, upper) * ACT[...]

    def step(s, carry):
        more = s + 1 < STEPS

        @pl.when(has_dn)
        def _():
            y_up(s).wait_recv()

        @pl.when(has_up)
        def _():
            y_down(s).wait_recv()

        @pl.when(has_hi)
        def _():
            for c in range(3):
                x_down(s, c, D.at[s, c, 0]).wait_recv()
            for c in range(3):
                last_layer(s, c)

            @pl.when(more)
            def _():
                for c in range(3):
                    x_up(s + 1, c, D.at[s + 1, c, last]).start()

        @pl.when(is_face)
        def _():
            for c in (1, 2):
                last_layer(s, c)
            for c in (1, 2):
                pack_face(s + 1, c)

            @pl.when(more)
            def _():
                for c in (1, 2):
                    send_face(s + 1, c)

        @pl.when(has_lo)
        def _():
            for c in range(3):
                x_up(s, c, D.at[s, c, last]).wait_recv()

        for c in range(3):
            first_layer(s, c)

        @pl.when(more & has_lo)
        def _():
            for c in range(3):
                x_down(s + 1, c, D.at[s + 1, c, 0]).start()

        @pl.loop(0, (last - 1) // 2)
        def _(pair):
            for offset in range(2):
                x = 2 * pair + 1 + offset
                for c in range(3):
                    here = D[s, c, x]
                    pull_x = SX[x + 1] * jnp.tanh(D[s, c, x + 1] - here)
                    below = PX[c]
                    PX[c] = pull_x
                    node_update(s, c, x, here, pull_x, below)

        @pl.when(more & has_up)
        def _():
            y_up(s + 1).start()

        @pl.when(more & has_dn)
        def _():
            y_down(s + 1).start()

        @pl.when(is_face)
        def _():
            for c in (1, 2):
                c_same(s, c).wait_recv()
                c_cross(s, c).wait_recv()
            weights(s)

            @pl.when(has_dn)
            def _():
                late_up(s).wait_recv()

            @pl.when(has_up)
            def _():
                late_down(s).wait_recv()

            own_x = own_face(s, 0) * depth
            c_same(s, 0).wait_recv()
            c_cross(s, 0).wait_recv()
            last_layer(s, 0, contact(s, own_x))

            pack_face(s + 1, 0)

            @pl.when(more)
            def _():
                send_face(s + 1, 0)
                send_late(s + 1)


        return carry

    lax.fori_loop(0, STEPS, step, 0)

    stores = [
        pltpu.make_async_copy(D.at[STEPS], out_d.at[0], out_sem.at[0]),
        pltpu.make_async_copy(V, out_v.at[0], out_sem.at[1]),
    ]
    for item in stores:
        item.start()

    @pl.when(has_hi)
    def _():
        m_x.wait_send()

    @pl.when(has_up)
    def _():
        m_y.wait_send()

    @pl.when(has_hi & has_up)
    def _():
        m_c.wait_send()

    def drain(s, carry):
        @pl.when(has_hi)
        def _():
            for c in range(3):
                x_up(s, c, D.at[s, c, last]).wait_send()

        @pl.when(has_lo)
        def _():
            for c in range(3):
                x_down(s, c, D.at[s, c, 0]).wait_send()

        @pl.when(has_up)
        def _():
            y_up(s).wait_send()

        @pl.when(has_dn)
        def _():
            y_down(s).wait_send()

        @pl.when(is_face)
        def _():
            for c in range(3):
                c_same(s, c).wait_send()
                c_cross(s, c).wait_send()

            @pl.when(has_up)
            def _():
                late_up(s).wait_send()

            @pl.when(has_dn)
            def _():
                late_down(s).wait_send()

        return carry

    lax.fori_loop(0, STEPS, drain, 0)
    for item in stores:
        item.wait()


def local(displacement, velocity, material, moduli, density, partner, active):
    length_x, length_y, length_z = displacement.shape[2:]
    count_x = lax.axis_size("gx")
    count_y = lax.axis_size("yz")
    f32 = jnp.float32
    i32 = jnp.int32
    layer = (length_y, length_z)
    solid = (length_x,) + layer
    anywhere = pl.BlockSpec(memory_space=pl.ANY)
    far_memory = pl.BlockSpec(memory_space=pltpu.HBM)
    dma = pltpu.SemaphoreType.DMA
    half = length_z // 2
    scaled_d, scaled_v = pl.pallas_call(
        functools.partial(kernel, count_x, count_y, (length_x, length_y, length_z)),
        out_shape=(
            jax.ShapeDtypeStruct(displacement.shape, f32),
            jax.ShapeDtypeStruct(velocity.shape, f32),
        ),
        in_specs=[far_memory] * 7,
        out_specs=(anywhere, anywhere),
        scratch_shapes=[
            pltpu.VMEM((STEPS + 1, 3) + solid, f32),
            pltpu.VMEM((3,) + solid, f32),
            pltpu.VMEM(solid, i32),
            pltpu.VMEM((length_x + 1, length_y + 8, length_z), f32),
            pltpu.VMEM((length_x + 1,) + layer, f32),
            pltpu.VMEM(solid, f32),
            pltpu.VMEM((length_x, length_z), f32),
            pltpu.VMEM(solid, f32),
            pltpu.VMEM(solid, f32),
            pltpu.VMEM(solid, f32),
            pltpu.VMEM((3,) + layer, f32),
            pltpu.VMEM((STEPS, 2, 3) + layer, f32),
            pltpu.VMEM((STEPS, 2, 3, length_x, length_z), f32),
            pltpu.VMEM((STEPS + 1, 2, 3, length_x, length_z), f32),
            pltpu.VMEM((STEPS, 2, 8, length_z), f32),
            pltpu.VMEM((STEPS + 1, 2, 8, length_z), f32),
            pltpu.VMEM(layer, i32),
            pltpu.VMEM((length_x, length_z), i32),
            pltpu.VMEM((8, length_z), i32),
            pltpu.VMEM((length_x, length_z), i32),
            pltpu.VMEM((STEPS + 1, 3) + layer, f32),
            pltpu.VMEM((STEPS, 3) + layer, f32),
            pltpu.VMEM((length_y, 2 * length_y), jnp.bfloat16),
            pltpu.VMEM((length_y, 2 * length_y), jnp.bfloat16),
            pltpu.VMEM(layer, f32),
            pltpu.VMEM((length_z, half, 2 * length_y), f32),
            pltpu.VMEM((3 * half, 2 * length_y), f32),
            pltpu.VMEM((3 * half, 2 * length_y), f32),
            pltpu.VMEM((3 * half, 2 * length_y), f32),
            pltpu.VMEM((2, length_z), i32),
            pltpu.VMEM((2, length_z), i32),
            pltpu.SMEM(moduli.shape, f32),
            pltpu.SMEM(density.shape, f32),
            dma((7,)), dma((2,)), dma((3,)), dma((3,)),
            dma((STEPS, 2, 3)), dma((STEPS, 2, 3)),
            dma((STEPS, 2)), dma((STEPS, 2)), dma((STEPS, 2)), dma((STEPS, 2)),
            dma((STEPS, 3, 2)), dma((STEPS, 3, 2)),
        ],
        compiler_params=pltpu.CompilerParams(
            collective_id=0, has_side_effects=True, vmem_limit_bytes=48 * 1024 * 1024
        ),
        name="impact",
    )(*[
        pltpu.with_memory_space_constraint(item, pltpu.HBM)
        for item in (
            displacement, velocity, material, moduli, density,
            partner.reshape(2, length_z), active.reshape(2, length_z),
        )
    ])
    return scaled_d * YIELD_SPAN, scaled_v * (YIELD_SPAN / STEP_TIME)


def solution(mesh):
    in_specs = (
        P("body", None, "gx", "yz", None),
        P("body", None, "gx", "yz", None),
        P("body", "gx", "yz", None),
        P(),
        P(),
        P(),
        P(),
    )
    out_specs = (P("body", None, "gx", "yz", None), P("body", None, "gx", "yz", None))
    return jax.shard_map(local, mesh=mesh, in_specs=in_specs, out_specs=out_specs, check_vma=False)
```

```python
import functools
import math

import jax
import jax.numpy as jnp
from jax import lax
from jax.experimental import pallas as pl
from jax.experimental.pallas import tpu as pltpu
from jax.sharding import PartitionSpec as P

STEPS = 4
STEP_TIME = 0.2
YIELD_SPAN = 0.5
PENALTY = 4.0
SOFT_WIDTH = 0.1
KERNEL_WIDTH = 1.5
LOG2E = 1.0 / math.log(2.0)
PLANE = math.sqrt(LOG2E / (2.0 * KERNEL_WIDTH * KERNEL_WIDTH))
GROUP = 16
LAYERS = 7

MESH = pl.DeviceIdType.MESH
HIGHEST = lax.Precision.HIGHEST


def kernel(
    count_x, count_y, dims,
    disp, velo, mat_hbm, moduli_hbm, density_hbm, partner_hbm, active_hbm,
    out_d, out_v,
    D, V, M, E, SX, SY, SYL, SZ, SZB, C, PX,
    XH, YH, YS, YLH, YLS, MX, MY, MC, MYS, CS, CP, GIVE, TAKE, ACT, WT, FY, FZ, FX,
    partner, active, moduli, density,
    load_sem, out_sem, m_send, m_recv, x_send, x_recv, y_send, y_recv, l_send, l_recv, c_send, c_recv,
):
    length_x, length_y, length_z = dims
    last = length_x - 1
    body = lax.axis_index("body")
    gx = lax.axis_index("gx")
    yz = lax.axis_index("yz")
    has_lo = gx > 0
    has_hi = gx < count_x - 1
    has_dn = yz > 0
    has_up = yz < count_y - 1
    is_face = gx == count_x - 1
    cross = lax.rem(yz + 1 - 2 * body + count_y, count_y)
    other = 1 - body

    quota = length_y // 2
    low = {"gx": gx - 1}
    high = {"gx": gx + 1}
    down = {"yz": yz - 1}
    up = {"yz": yz + 1}
    corner_up = {"gx": gx + 1, "yz": yz + 1}
    corner_dn = {"gx": gx - 1, "yz": yz - 1}
    same_peer = {"body": other}
    cross_peer = {"body": other, "yz": cross}

    row_id = lax.broadcasted_iota(jnp.int32, (length_y, length_z), 0)
    lane_id = lax.broadcasted_iota(jnp.int32, (length_y, length_z), 1)

    loads = [
        pltpu.make_async_copy(mat_hbm.at[0], M, load_sem.at[0]),
        pltpu.make_async_copy(disp.at[0], D.at[0], load_sem.at[1]),
        pltpu.make_async_copy(velo.at[0], V, load_sem.at[2]),
        pltpu.make_async_copy(moduli_hbm, moduli, load_sem.at[3]),
        pltpu.make_async_copy(density_hbm, density, load_sem.at[4]),
        pltpu.make_async_copy(partner_hbm, partner, load_sem.at[5]),
        pltpu.make_async_copy(active_hbm, active, load_sem.at[6]),
    ]
    for item in loads:
        item.start()

    barrier = pltpu.get_barrier_semaphore()

    def greet(condition, device):
        @pl.when(condition)
        def _():
            pl.semaphore_signal(barrier, inc=1, device_id=device, device_id_type=MESH)

    pairs = [
        (has_lo, low), (has_hi, high), (has_dn, down), (has_up, up),
        (has_hi & has_up, corner_up), (has_lo & has_dn, corner_dn),
        (is_face, same_peer), (is_face, cross_peer),
    ]
    for condition, device in pairs:
        greet(condition, device)
    pl.semaphore_wait(barrier, sum(condition.astype(jnp.int32) for condition, _ in pairs))

    def remote(source, target, send, recv, device):
        return pltpu.make_async_remote_copy(
            src_ref=source, dst_ref=target, send_sem=send, recv_sem=recv,
            device_id=device, device_id_type=MESH,
        )

    def x_up(s, c, source):
        return remote(source, XH.at[s, 0, c], x_send.at[s, 0, c], x_recv.at[s, 0, c], high)

    def x_down(s, c, source):
        return remote(source, XH.at[s, 1, c], x_send.at[s, 1, c], x_recv.at[s, 1, c], low)

    def late_up(s):
        return remote(YLS.at[s, 0], YLH.at[s, 0], l_send.at[s, 0], l_recv.at[s, 0], up)

    def late_down(s):
        return remote(YLS.at[s, 1], YLH.at[s, 1], l_send.at[s, 1], l_recv.at[s, 1], down)

    def y_up(s):
        return remote(YS.at[s, 0], YH.at[s, 0], y_send.at[s, 0], y_recv.at[s, 0], up)

    def y_down(s):
        return remote(YS.at[s, 1], YH.at[s, 1], y_send.at[s, 1], y_recv.at[s, 1], down)

    def c_same(s, c):
        return remote(
            CS.at[s, c, pl.ds(0, quota)], CP.at[s, c, pl.ds(0, quota)],
            c_send.at[s, c, 0], c_recv.at[s, c, 0], same_peer,
        )

    def c_cross(s, c):
        return remote(
            CS.at[s, c, pl.ds(quota, quota)], CP.at[s, c, pl.ds(quota, quota)],
            c_send.at[s, c, 1], c_recv.at[s, c, 1], cross_peer,
        )

    m_x = remote(mat_hbm.at[0, last], MX, m_send.at[0], m_recv.at[0], high)
    m_y = remote(MYS, MY, m_send.at[1], m_recv.at[1], up)
    m_c = remote(MYS.at[pl.ds(length_x - 8, 8)], MC, m_send.at[2], m_recv.at[2], corner_up)

    @pl.when(has_hi)
    def _():
        m_x.start()
        for c in range(3):
            x_up(0, c, disp.at[0, c, last]).start()

    @pl.when(has_lo)
    def _():
        for c in range(3):
            x_down(0, c, disp.at[0, c, 0]).start()

    half = length_z // 2
    low_lanes = lane_id < half

    def exact_pick(choice, value):
        high_part = value.astype(jnp.bfloat16)
        rest = value - high_part.astype(jnp.float32)
        middle = rest.astype(jnp.bfloat16)
        tail = (rest - middle.astype(jnp.float32)).astype(jnp.bfloat16)
        upper_parts = jnp.concatenate([high_part, middle], axis=0)
        lower_parts = jnp.concatenate([tail, jnp.zeros_like(tail)], axis=0)
        return jnp.dot(choice, upper_parts, preferred_element_type=jnp.float32) + jnp.dot(
            choice, lower_parts, preferred_element_type=jnp.float32
        )

    def turned_pair(value):
        turned = jnp.concatenate([value, value], axis=0).T
        return turned[:half], turned[half:]

    def own_face(s, c):
        lower, upper = turned_pair(D[s, c, last])
        return jnp.where(low_lanes, lower, upper)

    def pack_face(s, c):
        CS[s, c] = exact_pick(GIVE[...], D[s, c, last])

    def send_face(s, c):
        c_same(s, c).start()
        c_cross(s, c).start()

    @pl.when(jnp.logical_not(has_lo))
    def _():
        XH[:, 0] = jnp.zeros((STEPS, 3, length_y, length_z), jnp.float32)

    @pl.when(jnp.logical_not(has_hi))
    def _():
        XH[:, 1] = jnp.zeros((STEPS, 3, length_y, length_z), jnp.float32)

    @pl.when(jnp.logical_not(has_dn))
    def _():
        YH[:, 0] = jnp.zeros((STEPS, 3, length_x, length_z), jnp.float32)
        YLH[:, 0] = jnp.zeros((STEPS, 8, length_z), jnp.float32)
        MY[...] = jnp.zeros((length_x, length_z), jnp.int32)

    @pl.when(jnp.logical_not(has_up))
    def _():
        YH[:, 1] = jnp.zeros((STEPS, 3, length_x, length_z), jnp.float32)
        YLH[:, 1] = jnp.zeros((STEPS, 8, length_z), jnp.float32)

    @pl.when(jnp.logical_not(has_lo))
    def _():
        MX[...] = jnp.zeros((length_y, length_z), jnp.int32)

    @pl.when(jnp.logical_not(has_lo & has_dn))
    def _():
        MC[...] = jnp.zeros((8, length_z), jnp.int32)

    loads[0].wait()

    @pl.loop(0, length_x)
    def _(i):
        MYS[pl.ds(i, 1)] = M[i, pl.ds(length_y - 1, 1)]

    @pl.when(has_up)
    def _():
        m_y.start()

    @pl.when(has_hi & has_up)
    def _():
        m_c.start()

    for item in loads[3:]:
        item.wait()

    @pl.when(is_face)
    def _():
        base = yz * length_y
        size = (2 * length_y, 2 * length_y)
        rows = lax.broadcasted_iota(jnp.int32, size, 0)
        lanes = lax.broadcasted_iota(jnp.int32, size, 1)

        def publish(mate_col, mate_row, live):
            near_col = (mate_col >= base) & (mate_col < base + length_y)
            near_row = (mate_row >= base) & (mate_row < base + length_y)
            shift_col = jnp.where(near_col, 0.0, 1.0)
            shift_row = jnp.where(near_row, 0.0, 1.0)
            alike = shift_col == shift_row
            before = jnp.where(alike & (mate_row < mate_col) & (lanes < length_y), 1.0, 0.0)
            spot = jnp.sum(before, axis=1, keepdims=True) + quota * shift_col
            name = lanes.astype(jnp.float32)
            TAKE[...] = jnp.where(
                (name == spot) | (name == spot + float(length_y)), 1.0, 0.0
            )[:length_y].astype(jnp.bfloat16)
            earlier = jnp.where(alike & (rows < lanes) & (rows < length_y), 1.0, 0.0)
            slot = jnp.sum(earlier, axis=0, keepdims=True) + quota * shift_row
            single = jnp.where(rows.astype(jnp.float32) == slot, 1.0, 0.0)
            GIVE[...] = jnp.where(lanes < length_y, single, pltpu.roll(single, length_y, 1))[
                :length_y
            ].astype(jnp.bfloat16)
            ACT[...] = live[:length_y] * (-PENALTY * SOFT_WIDTH)

        @pl.when(body == 0)
        def _():
            def own_block(table):
                line = jnp.where(yz < 2, table[pl.ds(0, 1)], table[pl.ds(1, 1)])
                moved = jnp.where(lax.rem(yz, 2) == 0, line, pltpu.roll(line, half, 1))
                return jnp.broadcast_to(moved.astype(jnp.float32), size)

            across = own_block(partner)
            publish(across.T.astype(jnp.int32), across.astype(jnp.int32), own_block(active).T)

        @pl.when(body == 1)
        def _():
            mate = jnp.zeros((2 * length_y, 1), jnp.float32)
            live = jnp.zeros((2 * length_y, 1), jnp.float32)
            for part in range(2):
                hit = jnp.where(partner[pl.ds(part, 1)] == rows + base, 1.0, 0.0)
                name = (lanes + part * length_z).astype(jnp.float32)
                mate = mate + jnp.sum(hit * name, axis=1, keepdims=True)
                live = live + jnp.sum(
                    hit * active[pl.ds(part, 1)].astype(jnp.float32), axis=1, keepdims=True
                )
            down_rows = jnp.broadcast_to(mate, size)
            publish(
                down_rows.astype(jnp.int32), down_rows.T.astype(jnp.int32),
                jnp.broadcast_to(live, size),
            )

    loads[1].wait()

    @pl.loop(0, length_x)
    def _(i):
        for c in range(3):
            doubled = D[0, c, i] * (1.0 / YIELD_SPAN)
            D[0, c, i] = doubled
            YS[0, 0, c, pl.ds(i, 1)] = doubled[length_y - 1 :]
            YS[0, 1, c, pl.ds(i, 1)] = doubled[:1]

    def send_late(s):
        @pl.when(has_up)
        def _():
            late_up(s).start()

        @pl.when(has_dn)
        def _():
            late_down(s).start()

    @pl.when(is_face)
    def _():
        YLS[0, 0, pl.ds(0, 1)] = D[0, 0, last, pl.ds(length_y - 1, 1)]
        YLS[0, 1, pl.ds(0, 1)] = D[0, 0, last, pl.ds(0, 1)]
        send_late(0)
        for c in (1, 2, 0):
            pack_face(0, c)
        for c in (1, 2, 0):
            send_face(0, c)

    @pl.when(has_up)
    def _():
        y_up(0).start()

    @pl.when(has_dn)
    def _():
        y_down(0).start()

    def lookup(kinds, table):
        result = jnp.full(kinds.shape, table[0], jnp.float32)
        for kind in range(1, 8):
            result = jnp.where(kinds == kind, table[kind], result)
        return result

    inner_lane = lane_id < length_z - 1
    own_edge = inner_lane & jnp.logical_or(has_up, row_id < length_y - 1)

    @pl.loop(0, length_x)
    def _(i):
        kinds = M[i]
        keep = own_edge & (jnp.logical_or(has_hi, i < last))
        E[i + 1, pl.ds(8, length_y)] = jnp.where(keep, lookup(kinds, moduli), 0.0)
        C[i] = (STEP_TIME * STEP_TIME / YIELD_SPAN) / lookup(kinds, density)

    @pl.when(has_lo)
    def _():
        m_x.wait_recv()

    @pl.when(has_dn)
    def _():
        m_y.wait_recv()

    @pl.when(has_lo & has_dn)
    def _():
        m_c.wait_recv()

    E[0, pl.ds(8, length_y)] = jnp.where(own_edge & has_lo, lookup(MX[...], moduli), 0.0)
    row_lane = lax.broadcasted_iota(jnp.int32, (length_x, length_z), 1) < length_z - 1
    row_pos = lax.broadcasted_iota(jnp.int32, (length_x, length_z), 0)
    side = jnp.where(
        row_lane & has_dn & jnp.logical_or(has_hi, row_pos < last), lookup(MY[...], moduli), 0.0
    )
    SYL[...] = side
    E[0, pl.ds(7, 1)] = jnp.where(
        inner_lane[:1] & has_lo & has_dn, lookup(MC[pl.ds(7, 1)], moduli), 0.0
    )

    @pl.loop(0, length_x)
    def _(i):
        E[i + 1, pl.ds(7, 1)] = SYL[pl.ds(i, 1)]

    def with_left(value):
        return value + pltpu.roll(value, 1, 1)

    quarter = 0.25 * YIELD_SPAN

    @pl.loop(0, length_x + 1)
    def _(i):
        whole = E[i]
        here = whole[8:]
        behind = pltpu.roll(whole, 1, 0)[8:]
        SX[i] = quarter * with_left(here + behind)

        @pl.when(i > 0)
        def _():
            under = E[i - 1]
            both = whole + under
            SY[i - 1] = quarter * with_left(both[8:])
            edge = quarter * (both + pltpu.roll(both, 1, 0))[8:]
            SZ[i - 1] = edge
            SZB[i - 1] = pltpu.roll(edge, 1, 1)
            SYL[pl.ds(i - 1, 1)] = quarter * with_left(both[7:8])

    loads[2].wait()

    @pl.loop(0, length_x)
    def _(i):
        for c in range(3):
            V[c, i] = V[c, i] * (STEP_TIME / YIELD_SPAN)

    def node_update(s, c, x, here, pull_x, pull_x_below, push=None):
        if push is None:
            row_up, row_down = YH[s, 1, c, pl.ds(x, 1)], YH[s, 0, c, pl.ds(x, 1)]
        else:
            row_up, row_down = YLH[s, 1, pl.ds(0, 1)], YLH[s, 0, pl.ds(0, 1)]
        ahead = pltpu.roll(here, length_y - 1, 0)
        ahead = jnp.where(row_id == length_y - 1, row_up, ahead)
        pull_y = SY[x] * jnp.tanh(ahead - here)
        first = SYL[pl.ds(x, 1)] * jnp.tanh(here[:1] - row_down)
        below = jnp.where(row_id == 0, first, pltpu.roll(pull_y, 1, 0))
        pull_z = SZ[x] * jnp.tanh(pltpu.roll(here, length_z - 1, 1) - here)
        pull_z_below = SZB[x] * jnp.tanh(here - pltpu.roll(here, 1, 1))
        force = (pull_x - pull_x_below) + (pull_y - below) + (pull_z - pull_z_below)
        if push is not None:
            force = force + push
        speed = V[c, x] + C[x] * force
        V[c, x] = speed
        moved = here + speed
        D[s + 1, c, x] = moved
        if push is None:
            YS[s + 1, 0, c, pl.ds(x, 1)] = moved[length_y - 1 :]
            YS[s + 1, 1, c, pl.ds(x, 1)] = moved[:1]
        else:
            YLS[s + 1, 0, pl.ds(0, 1)] = moved[length_y - 1 :]
            YLS[s + 1, 1, pl.ds(0, 1)] = moved[:1]

    def raw_scale(s):
        return jnp.where(s == 0, 1.0 / YIELD_SPAN, 1.0)

    def first_layer(s, c):
        here = D[s, c, 0]
        pull_below = SX[0] * jnp.tanh(here - XH[s, 0, c] * raw_scale(s))
        pull_x = SX[1] * jnp.tanh(D[s, c, 1] - here)
        PX[c] = pull_x
        node_update(s, c, 0, here, pull_x, pull_below)

    def last_layer(s, c, push=None):
        here = D[s, c, last]
        pull_below = SX[last] * jnp.tanh(here - D[s, c, last - 1])
        pull_x = SX[last + 1] * jnp.tanh(XH[s, 1, c] * raw_scale(s) - here)
        node_update(s, c, last, here, pull_x, pull_below, push)

    def matched(s, c):
        return turned_pair(exact_pick(TAKE[...], CP[s, c]))

    def spread(ref, lower, upper):
        near = jnp.where(low_lanes, lower, upper)
        other_half = jnp.where(low_lanes, upper, lower)
        ref[pl.ds(0, half)] = near
        ref[pl.ds(half, half)] = other_half
        ref[pl.ds(2 * half, half)] = near

    row_place = row_id.astype(jnp.float32)
    place = row_place + jnp.where(low_lanes, 0.0, float(half))
    depth = LOG2E / SOFT_WIDTH * YIELD_SPAN

    def weights(s):
        lower, upper = matched(s, 1)
        spread(FY, lower * (PLANE * YIELD_SPAN), upper * (PLANE * YIELD_SPAN))
        lower, upper = matched(s, 2)
        spread(
            FZ,
            (lower * YIELD_SPAN + row_place) * PLANE,
            (upper * YIELD_SPAN + (row_place + float(half))) * PLANE,
        )
        own_y = own_face(s, 1) * (PLANE * YIELD_SPAN)
        own_z = (own_face(s, 2) * YIELD_SPAN + place) * PLANE

        @pl.loop(0, length_z // GROUP)
        def _(block):
            for k in range(GROUP):
                turn = block * GROUP + k
                along_y = own_y - FY[pl.ds(turn, half)]
                along_z = own_z - FZ[pl.ds(turn, half)]
                WT[turn] = jnp.exp2((0.0 - along_y * along_y) - along_z * along_z)

    def contact(s, own_x):
        lower, upper = matched(s, 0)
        spread(FX, lower * depth, upper * depth)

        def group(block, total):
            for k in range(GROUP):
                turn = block * GROUP + k
                squeeze = own_x + FX[pl.ds(turn, half)]
                soft = jnp.log(1.0 + jnp.exp2(jnp.minimum(squeeze, 64.0)))
                total = total + WT[turn] * jnp.maximum(soft, squeeze * math.log(2.0))
            return total

        total = lax.fori_loop(
            0, length_z // GROUP, group, jnp.zeros((half, length_z), jnp.float32)
        )
        lower, upper = turned_pair(total)
        return jnp.where(low_lanes, lower, upper) * ACT[...]

    def step(s, carry):
        more = s + 1 < STEPS

        @pl.when(has_dn)
        def _():
            y_up(s).wait_recv()

        @pl.when(has_up)
        def _():
            y_down(s).wait_recv()

        @pl.when(has_hi)
        def _():
            for c in range(3):
                x_down(s, c, D.at[s, c, 0]).wait_recv()
            for c in range(3):
                last_layer(s, c)

            @pl.when(more)
            def _():
                for c in range(3):
                    x_up(s + 1, c, D.at[s + 1, c, last]).start()

        @pl.when(is_face)
        def _():
            for c in (1, 2):
                last_layer(s, c)
            for c in (1, 2):
                pack_face(s + 1, c)

        @pl.when(has_lo)
        def _():
            for c in range(3):
                x_up(s, c, D.at[s, c, last]).wait_recv()

        for c in range(3):
            first_layer(s, c)

        @pl.when(more & has_lo)
        def _():
            for c in range(3):
                x_down(s + 1, c, D.at[s + 1, c, 0]).start()

        @pl.loop(0, (last - 1) // LAYERS)
        def _(pack):
            for offset in range(LAYERS):
                x = LAYERS * pack + 1 + offset
                for c in range(3):
                    here = D[s, c, x]
                    pull_x = SX[x + 1] * jnp.tanh(D[s, c, x + 1] - here)
                    below = PX[c]
                    PX[c] = pull_x
                    node_update(s, c, x, here, pull_x, below)

        @pl.when(more & has_up)
        def _():
            y_up(s + 1).start()

        @pl.when(more & has_dn)
        def _():
            y_down(s + 1).start()

        @pl.when(is_face)
        def _():
            for c in (1, 2):
                c_same(s, c).wait_recv()
                c_cross(s, c).wait_recv()
            weights(s)

            @pl.when(has_dn)
            def _():
                late_up(s).wait_recv()

            @pl.when(has_up)
            def _():
                late_down(s).wait_recv()

            @pl.when(more)
            def _():
                for c in (1, 2):
                    send_face(s + 1, c)

            own_x = own_face(s, 0) * depth
            c_same(s, 0).wait_recv()
            c_cross(s, 0).wait_recv()
            last_layer(s, 0, contact(s, own_x))

            pack_face(s + 1, 0)

            @pl.when(more)
            def _():
                send_face(s + 1, 0)
                send_late(s + 1)


        return carry

    lax.fori_loop(0, STEPS, step, 0)

    stores = [
        pltpu.make_async_copy(D.at[STEPS], out_d.at[0], out_sem.at[0]),
        pltpu.make_async_copy(V, out_v.at[0], out_sem.at[1]),
    ]
    for item in stores:
        item.start()

    @pl.when(has_hi)
    def _():
        m_x.wait_send()

    @pl.when(has_up)
    def _():
        m_y.wait_send()

    @pl.when(has_hi & has_up)
    def _():
        m_c.wait_send()

    def drain(s, carry):
        @pl.when(has_hi)
        def _():
            for c in range(3):
                x_up(s, c, D.at[s, c, last]).wait_send()

        @pl.when(has_lo)
        def _():
            for c in range(3):
                x_down(s, c, D.at[s, c, 0]).wait_send()

        @pl.when(has_up)
        def _():
            y_up(s).wait_send()

        @pl.when(has_dn)
        def _():
            y_down(s).wait_send()

        @pl.when(is_face)
        def _():
            for c in range(3):
                c_same(s, c).wait_send()
                c_cross(s, c).wait_send()

            @pl.when(has_up)
            def _():
                late_up(s).wait_send()

            @pl.when(has_dn)
            def _():
                late_down(s).wait_send()

        return carry

    lax.fori_loop(0, STEPS, drain, 0)
    for item in stores:
        item.wait()


def local(displacement, velocity, material, moduli, density, partner, active):
    length_x, length_y, length_z = displacement.shape[2:]
    count_x = lax.axis_size("gx")
    count_y = lax.axis_size("yz")
    f32 = jnp.float32
    i32 = jnp.int32
    layer = (length_y, length_z)
    solid = (length_x,) + layer
    anywhere = pl.BlockSpec(memory_space=pl.ANY)
    far_memory = pl.BlockSpec(memory_space=pltpu.HBM)
    dma = pltpu.SemaphoreType.DMA
    half = length_z // 2
    scaled_d, scaled_v = pl.pallas_call(
        functools.partial(kernel, count_x, count_y, (length_x, length_y, length_z)),
        out_shape=(
            jax.ShapeDtypeStruct(displacement.shape, f32),
            jax.ShapeDtypeStruct(velocity.shape, f32),
        ),
        in_specs=[far_memory] * 7,
        out_specs=(anywhere, anywhere),
        scratch_shapes=[
            pltpu.VMEM((STEPS + 1, 3) + solid, f32),
            pltpu.VMEM((3,) + solid, f32),
            pltpu.VMEM(solid, i32),
            pltpu.VMEM((length_x + 1, length_y + 8, length_z), f32),
            pltpu.VMEM((length_x + 1,) + layer, f32),
            pltpu.VMEM(solid, f32),
            pltpu.VMEM((length_x, length_z), f32),
            pltpu.VMEM(solid, f32),
            pltpu.VMEM(solid, f32),
            pltpu.VMEM(solid, f32),
            pltpu.VMEM((3,) + layer, f32),
            pltpu.VMEM((STEPS, 2, 3) + layer, f32),
            pltpu.VMEM((STEPS, 2, 3, length_x, length_z), f32),
            pltpu.VMEM((STEPS + 1, 2, 3, length_x, length_z), f32),
            pltpu.VMEM((STEPS, 2, 8, length_z), f32),
            pltpu.VMEM((STEPS + 1, 2, 8, length_z), f32),
            pltpu.VMEM(layer, i32),
            pltpu.VMEM((length_x, length_z), i32),
            pltpu.VMEM((8, length_z), i32),
            pltpu.VMEM((length_x, length_z), i32),
            pltpu.VMEM((STEPS + 1, 3) + layer, f32),
            pltpu.VMEM((STEPS, 3) + layer, f32),
            pltpu.VMEM((length_y, 2 * length_y), jnp.bfloat16),
            pltpu.VMEM((length_y, 2 * length_y), jnp.bfloat16),
            pltpu.VMEM(layer, f32),
            pltpu.VMEM((length_z, half, 2 * length_y), f32),
            pltpu.VMEM((3 * half, 2 * length_y), f32),
            pltpu.VMEM((3 * half, 2 * length_y), f32),
            pltpu.VMEM((3 * half, 2 * length_y), f32),
            pltpu.VMEM((2, length_z), i32),
            pltpu.VMEM((2, length_z), i32),
            pltpu.SMEM(moduli.shape, f32),
            pltpu.SMEM(density.shape, f32),
            dma((7,)), dma((2,)), dma((3,)), dma((3,)),
            dma((STEPS, 2, 3)), dma((STEPS, 2, 3)),
            dma((STEPS, 2)), dma((STEPS, 2)), dma((STEPS, 2)), dma((STEPS, 2)),
            dma((STEPS, 3, 2)), dma((STEPS, 3, 2)),
        ],
        compiler_params=pltpu.CompilerParams(
            collective_id=0, has_side_effects=True, vmem_limit_bytes=48 * 1024 * 1024
        ),
        name="impact",
    )(*[
        pltpu.with_memory_space_constraint(item, pltpu.HBM)
        for item in (
            displacement, velocity, material, moduli, density,
            partner.reshape(2, length_z), active.reshape(2, length_z),
        )
    ])
    return scaled_d * YIELD_SPAN, scaled_v * (YIELD_SPAN / STEP_TIME)


def solution(mesh):
    in_specs = (
        P("body", None, "gx", "yz", None),
        P("body", None, "gx", "yz", None),
        P("body", "gx", "yz", None),
        P(),
        P(),
        P(),
        P(),
    )
    out_specs = (P("body", None, "gx", "yz", None), P("body", None, "gx", "yz", None))
    return jax.shard_map(local, mesh=mesh, in_specs=in_specs, out_specs=out_specs, check_vma=False)
```
